32 devices in a mesh: row: 4 (over y, x), col: 4 (over z), depth: 2 (over core).
Axes of the slice: x: 2, y: 2, z: 4, core: 2. Of those that a mesh axis runs over, the one named last changes fastest.
Arguments:
- blocks: float32 [24, 4, 6, 128, 128], P('row', 'col'), may hold values from -1.2 to 1.2
- columns: int32 [24, 4, 6], P('row', 'col'), may hold values from 0 to 23, as said below
- branch: int32 [24], P('row'), may hold values 0 or 1
Outputs:
- updated: float32 [24, 4, 6, 128, 128], P('row', 'col')
- traces: float32 [2], replicated
The draws below stay inside these ranges and needn't reach their ends.
Inputs may be any that keep to these rules, and one draw needn't show every extreme that they name: Each block row names 6 distinct block columns in each column group g, all within g * 6 to (g + 1) * 6 - 1, and block row i names column i. `branch`: 1 selects the square for that block row, 0 selects 2 X minus the square.
All inputs are finite; a program needn't handle non-finite values.
Results may differ from the reference program's by a relative error of at most 0.0003.
Values sent between devices are 32-bit elements; how exact they have to be, the bound alone decides.
A program may use at most 64 MiB of HBM per device.

```python
import jax
import jax.numpy as jnp
from jax import lax

BS = 128
SPG = 6
CGROUPS = 4
NB = 24
COLGRP = 6


def draw_columns(key, part):
    key_list = jax.random.split(key, NB * CGROUPS)
    row_ids = jnp.repeat(jnp.arange(NB, dtype=jnp.int32), CGROUPS)
    group_ids = jnp.tile(jnp.arange(CGROUPS, dtype=jnp.int32), NB)

    def pick(single_key, row_id, group_id):
        shuffled = jax.random.permutation(single_key, COLGRP)
        placed = jnp.argsort(shuffled)
        local_ids = jnp.arange(COLGRP, dtype=jnp.int32)
        scores = jnp.where(local_ids + group_id * COLGRP == row_id, -1, placed)
        chosen = jnp.argsort(scores)[:SPG]
        return (chosen + group_id * COLGRP).astype(jnp.int32)
    return jax.vmap(pick)(key_list, row_ids, group_ids).reshape(NB, CGROUPS, SPG)


def touch_ends(array, own_key, smallest, top_value):
    spot = [jax.random.randint(jax.random.fold_in(own_key, axis), (), 0, length) for axis, length in enumerate(array.shape)]
    longest = array.shape.index(max(array.shape))
    next_to = spot[:longest] + [(spot[longest] + 1) % array.shape[longest]] + spot[longest + 1:]
    return array.at[tuple(spot)].set(smallest).at[tuple(next_to)].set(top_value)


def steps_of(rng, shape, pieces, smallest, largest):
    loudness = 1.0
    for axis_at, shards_of in pieces:
        steps = jax.random.uniform(jax.random.fold_in(jax.random.fold_in(rng, 6), axis_at), (shards_of,), jnp.float32, smallest / len(pieces), largest / len(pieces))
        loudness = loudness * jnp.repeat(jnp.exp(steps), shape[axis_at] // shards_of).reshape((-1,) + (1,) * (len(shape) - 1 - axis_at))
    return loudness


def noise(key, shape, width, reach, cuts=(), kind=jnp.bfloat16):
    loudness = steps_of(key, shape, cuts, -0.22, 0.18) if cuts else 1.0
    array = jax.random.normal(key, shape, jnp.float32) * width * loudness
    return jnp.minimum(jnp.maximum(array, -reach), reach).astype(kind)


def setup_inputs(seed: int = 0) -> dict:
    arg_keys = jax.random.split(jax.random.key(seed), 4)
    return {
        "blocks": noise(arg_keys[0], (NB, CGROUPS, SPG, BS, BS), 0.2, 1.2, ((0, 4), (1, 4)), jnp.float32),
        "columns": draw_columns(jax.random.fold_in(arg_keys[3], 71), 0),
        "branch": touch_ends((jax.random.randint(arg_keys[2], (NB,), 0, 2) < 1).astype(jnp.int32), jax.random.fold_in(arg_keys[2], 1), 0, 1),
    }


EXACT = lax.Precision.HIGHEST


def reference(blocks, columns, branch):
    slot_total = CGROUPS * SPG
    flat_cols = columns.reshape(NB, slot_total)
    flat_blocks = blocks.reshape(NB, slot_total, BS, BS)

    def one_row(row_id):
        own_cols = columns[row_id]
        inner_ids = flat_cols[row_id]
        far_blocks = blocks[inner_ids]
        far_cols = columns[inner_ids]
        matches = (far_cols[:, :, :, None] == own_cols[None, :, None, :]).astype(jnp.float32)
        chosen = jnp.einsum("sgbj,sgbxy->sgjxy", matches, far_blocks, precision=EXACT)
        return jnp.einsum("sxy,sgjyz->gjxz", flat_blocks[row_id], chosen, precision=EXACT)

    product = lax.map(one_row, jnp.arange(NB, dtype=jnp.int32))
    chooser = (branch == 1)[:, None, None, None, None]
    updated = jnp.where(chooser, product, 2.0 * blocks - product)
    row_ids = jnp.arange(NB, dtype=jnp.int32)[:, None, None]
    on_diag = (columns == row_ids).astype(jnp.float32)
    old_term = jnp.sum(on_diag * jnp.trace(blocks, axis1=3, axis2=4))
    new_term = jnp.sum(on_diag * jnp.trace(updated, axis1=3, axis2=4))
    return updated, jnp.stack([old_term, new_term])
```

```python
import functools

import jax
import jax.numpy as jnp
from jax import lax
from jax.experimental import pallas as pl
from jax.experimental.pallas import tpu as pltpu
from jax.sharding import PartitionSpec as P

BS = 128
SPG = 6


EXACT = lax.Precision.HIGHEST


def shifted(value, axis, steps):
    count = lax.axis_size(axis)
    pairs = [(source, (source + steps) % count) for source in range(count)]
    return lax.ppermute(value, axis, pairs)


def cannon_sum(a_blocks, a_cols, out_cols, moving, moving_cols, offset, panel, passer):
    grid_rows = lax.axis_size("row")
    my_row = lax.axis_index("row")
    out_count = a_blocks.shape[0]
    slot_total = a_blocks.shape[1] * a_blocks.shape[2]
    a_flat = a_blocks.reshape(out_count, slot_total, BS, BS)
    a_cflat = a_cols.reshape(out_count, slot_total)
    tile_rows = moving.shape[0]
    start_sum = jnp.zeros((out_count, SPG, BS, BS), jnp.float32)

    def contribute(running, pieces, piece_cols, step_index):
        source = (my_row - step_index) % grid_rows
        wanted = source * panel + offset + jnp.arange(tile_rows, dtype=jnp.int32)
        hits = (a_cflat[:, :, None] == wanted[None, None, :]).astype(jnp.float32)
        stacked = jnp.einsum("nst,nsxy->tnxy", hits, a_flat, precision=EXACT)
        matches = (piece_cols[:, None, None, :] == out_cols[None, :, :, None]).astype(jnp.float32)

        def one_tile_row(total, items):
            left_side, right_side, pairing = items
            products = jnp.einsum("nxy,byz->nbxz", left_side, right_side, precision=EXACT)
            return (total + jnp.einsum("njb,nbxz->njxz", pairing, products, precision=EXACT), 0)

        running, unused = lax.scan(one_tile_row, running, (stacked, pieces, matches))
        return running

    def turn(step_index, carry):
        running, pieces, piece_cols = carry
        running = contribute(running, pieces, piece_cols, step_index)
        pieces, piece_cols = passer(pieces, piece_cols)
        return (running, pieces, piece_cols)

    running, pieces, piece_cols = lax.fori_loop(
        0, grid_rows - 1, turn, (start_sum, moving, moving_cols)
    )
    return contribute(running, pieces, piece_cols, grid_rows - 1)


def pass_whole(pieces, piece_cols):
    return shifted((pieces, piece_cols), "row", 1)


def on_device(blocks, columns, branch):
    panel = blocks.shape[0]
    layer_count = lax.axis_size("depth")
    layer = lax.axis_index("depth")
    my_row = lax.axis_index("row")
    rows_half = panel // layer_count
    first_row = layer * rows_half
    own_blocks = blocks[:, 0]
    own_cols = columns[:, 0]
    half_blocks = lax.dynamic_slice_in_dim(blocks, first_row, rows_half, 0)
    half_cols = lax.dynamic_slice_in_dim(columns, first_row, rows_half, 0)
    a_blocks, a_cols = (
        lax.all_gather(half_blocks, "col", axis=1, tiled=True),
        lax.all_gather(half_cols, "col", axis=1, tiled=True),
    )
    partial_sum = cannon_sum(
        a_blocks, a_cols, half_cols[:, 0], own_blocks, own_cols, 0, panel, pass_whole
    )
    product = lax.all_gather(partial_sum, "depth", axis=0, tiled=True)
    chooser = (branch == 1)[:, None, None, None]
    updated = jnp.where(chooser, product, 2.0 * own_blocks - product)
    row_ids = my_row * panel + jnp.arange(panel, dtype=jnp.int32)
    on_diag = (own_cols == row_ids[:, None]).astype(jnp.float32)
    old_term = jnp.sum(on_diag * jnp.trace(own_blocks, axis1=2, axis2=3))
    new_term = jnp.sum(on_diag * jnp.trace(updated, axis1=2, axis2=3))
    traces = lax.psum(jnp.stack([old_term, new_term]), ("row", "col"))
    return (updated[:, None], traces)


MESH = pl.DeviceIdType.MESH
PIECES = 6
WHOLE = 2
CHUNKS = 3


def halves(value):
    high = value.astype(jnp.bfloat16)
    return high, (value - high.astype(jnp.float32)).astype(jnp.bfloat16)


def square_kernel(
    cols_ref, branch_ref, blocks_hbm, out_ref, trace_ref,
    mine, others, tile, left, right, extra, high_ref, low_ref, total, partial, partial_in, pair, parts,
    in_sem, cross_s, cross_r, up_s, up_r, down_s, down_r, part_s, part_r,
    near_s, near_r, far_s, far_r, give_s, give_r, lift_s, lift_r,
    near_ss, near_sr, far_ss, far_sr, give_ss, give_sr, own_ss, own_sr, lift_ss, lift_sr,
    out_s, out_r, pair_s, pair_r, t_send, t_recv, ready,
):
    row, col, depth = lax.axis_index("row"), lax.axis_index("col"), lax.axis_index("depth")
    panel, slots = 2 * mine.shape[0], mine.shape[1]
    groups = parts.shape[0]
    size = tile.shape[0]
    half = size // 2
    piece = half // PIECES
    per_block = BS // piece
    side = col // 2

    def mirrored(value):
        return value + side * (3 - 2 * value)

    mrow, mcol = mirrored(row), mirrored(col)
    outer = mcol == 0
    end, mid, mid2, end2 = mirrored(0), mirrored(1), mirrored(2), mirrored(3)
    group1 = jnp.where(mrow == 0, end2, mid2)
    group2 = jnp.where(mrow == 0, mid2, end2)
    direct = jnp.where(mrow < 2, group1, mid)
    summed = jnp.where(mrow < 2, mid, group1)
    x_row, y_row, corner = row + 1 - 2 * (row % 2), (row + 2) % 4, 3 - row
    mrow_x, mrow_y = mrow + 1 - 2 * (mrow % 2), (mrow + 2) % 4
    beside = (x_row, y_row)
    sibling = (row, col, 1 - depth)
    plane = ((x_row, col, depth), (y_row, col, depth))
    partner = (row, col + 1 - 2 * (col % 2), depth)
    opposite = (row, 3 - col, depth)

    barrier = pltpu.get_barrier_semaphore()
    for peer in (sibling,) + plane + (partner,):
        pl.semaphore_signal(barrier, inc=1, device_id=peer, device_id_type=MESH)

    @pl.when(jnp.logical_not(outer))
    def _():
        pl.semaphore_signal(barrier, inc=1, device_id=opposite, device_id_type=MESH)

    def incoming(turn):
        block = 2 * (turn % CHUNKS) + (depth + turn // CHUNKS) % 2
        place = mine if turn < CHUNKS else others
        return block, pltpu.make_async_copy(blocks_hbm.at[block, 0], place.at[turn % CHUNKS], in_sem.at[turn])

    def ordered(turn):
        block = incoming(turn)[0]
        place = mine if turn < CHUNKS else others
        at = pl.ds(pl.multiple_of(block * BS, BS), BS)
        for target_slot in range(slots):
            source = 0
            for slot in range(1, slots):
                source = jnp.where(lax.rem(cols_ref[block, 0, slot], slots) == target_slot, slot, source)
            value = place[turn % CHUNKS, source]
            tile[at, target_slot * BS:(target_slot + 1) * BS] = value
            if turn < CHUNKS:
                left[col, turn * BS:(turn + 1) * BS, target_slot * BS:(target_slot + 1) * BS] = value

    def take_blocks(turns):
        for turn in turns:
            incoming(turn)[1].wait()
        for turn in turns:
            ordered(turn)

    for turn in range(panel):
        incoming(turn)[1].start()
    take_blocks(range(CHUNKS))
    pl.semaphore_wait(barrier, jnp.where(outer, 4, 5))

    def copy(src, dst, send, recv, target):
        return pltpu.make_async_remote_copy(
            src_ref=src, dst_ref=dst, send_sem=send, recv_sem=recv, device_id=target, device_id_type=MESH
        )

    def some(index, count=1):
        return pl.ds(pl.multiple_of(index * piece, piece), count * piece)

    def spot(index, core):
        start = (2 * (index // per_block) + core) * BS + (index % per_block) * piece
        return pl.ds(pl.multiple_of(start, piece), piece)

    def chunk(index, core):
        return pl.ds(pl.multiple_of((2 * index + core) * BS, BS), BS)

    def cross(which, index):
        place = left.at[col if which == 0 else end, some(index)]
        return copy(place, place, cross_s.at[which, index], cross_r.at[which, index], opposite)

    def cross_in(second, index):
        which = jnp.where((mrow == 0) != second, 1, 0)
        place = left.at[group2 if second else group1, some(index)]
        return copy(place, place, cross_s.at[which, index], cross_r.at[which, index], sibling)

    def up(index):
        place = left.at[end, some(index)]
        return copy(place, place, up_s.at[index], up_r.at[index], partner)

    def down(which, index):
        place = left.at[(mid, group1, group2)[which], some(index)]
        return copy(place, place, down_s.at[which, index], down_r.at[which, index], partner)

    def goes_down(which, index):
        whole = index < WHOLE
        if which == 2:
            return whole
        return jnp.logical_or(whole, mrow >= 2 if which == 0 else mrow < 2)

    def down_part(index):
        at = some(index)
        return copy(partial.at[at], partial_in.at[at], part_s.at[index], part_r.at[index], partner)

    def near(axis, index):
        at = chunk(index, depth)
        return copy(tile.at[at], right.at[row, at], near_s.at[axis, index], near_r.at[axis, index], plane[axis])

    def near_place(axis, index, core):
        place = right.at[beside[axis], chunk(index, core)]
        return place, copy(place, place, near_ss.at[axis, index], near_sr.at[axis, index], sibling)

    def through_x(who):
        return jnp.where(outer, 2, jnp.where(who == 0, 1, jnp.where(who == 1, CHUNKS, 0)))

    def far(axis, index):
        place = right.at[beside[1 - axis], chunk(index, depth)]
        return copy(place, place, far_s.at[axis, index], far_r.at[index], plane[axis])

    def goes_far(axis, index):
        return index < through_x(mrow_x) if axis == 0 else index >= through_x(mrow_y)

    def far_place(index, core):
        place = right.at[corner, chunk(index, core)]
        return place, copy(place, place, far_ss.at[index], far_sr.at[index], sibling)

    def take_near(axis, index, forward=True):
        place, share = near_place(axis, index, depth)
        copy(place, place, near_s.at[axis, index], near_r.at[axis, index], sibling).wait_recv()
        share.start()
        if forward:
            pass_far(1 - axis, index)

    def pass_far(axis, index):
        @pl.when(goes_far(axis, index))
        def _():
            far(axis, index).start()

    def take_far(index):
        place, share = far_place(index, depth)
        copy(place, place, far_s.at[0, index], far_r.at[index], sibling).wait_recv()
        share.start()

    x_slot = jnp.where(mrow == 2, 1, 0)
    x_slot_there = jnp.where(mrow_x == 2, 1, 0)
    own_slot = jnp.where(mrow == 3, 1, 0)

    def give(axis, index):
        slot = x_slot_there if axis == 0 else 1
        return copy(
            left.at[end, some(index)], extra.at[slot, spot(index, depth)],
            give_s.at[axis, index], give_r.at[axis, index], plane[axis],
        )

    def gives(axis, index):
        if axis == 0:
            return mrow != 0
        return jnp.logical_or(mrow == 3, jnp.logical_and(mrow == 2, index < 2 * per_block))

    def given(axis, index):
        if axis == 0:
            return mrow != 1
        return jnp.logical_or(mrow == 1, jnp.logical_and(mrow == 0, index < 2 * per_block))

    def give_place(axis, index, core):
        place = extra.at[x_slot if axis == 0 else 1, spot(index, core)]
        return place, copy(place, place, give_ss.at[axis, index], give_sr.at[axis, index], sibling)

    def take_given(axis, index):
        @pl.when(given(axis, index))
        def _():
            place, share = give_place(axis, index, depth)
            copy(place, place, give_s.at[axis, index], give_r.at[axis, index], sibling).wait_recv()
            share.start()

    def own_share(index, core):
        return copy(
            left.at[end, some(index)], extra.at[own_slot, spot(index, core)],
            own_ss.at[index], own_sr.at[index], sibling,
        )

    def lift():
        at = chunk(CHUNKS - 1, depth)
        return copy(right.at[y_row, at], extra.at[1, at], lift_s.at[0], lift_r.at[0], partner)

    def lift_place(core):
        place = extra.at[1, chunk(CHUNKS - 1, core)]
        return place, copy(place, place, lift_ss.at[0], lift_sr.at[0], sibling)

    def split(source, slot, begin, count):
        def one(part, carry):
            at = pl.ds(pl.multiple_of((begin + part) * BS, BS), BS)
            high_ref[slot, at], low_ref[slot, at] = halves(source[at])
            return carry
        lax.fori_loop(0, count, one, 0)

    dot = functools.partial(jnp.dot, preferred_element_type=jnp.float32)

    def times(value, slot, at):
        high, low = halves(value)
        return (dot(high, low_ref[slot, at]) + dot(low, high_ref[slot, at])) + dot(high, high_ref[slot, at])

    everything = pl.ds(0, size)

    def accumulate(group, begin, count, at=everything):
        def one(part, carry):
            rows = pl.ds(pl.multiple_of((begin + part) * BS, BS), BS)
            result = times(left[group, rows, at], group, at)
            for slot in range(slots):
                total[slot, rows] += result[:, slot * BS:(slot + 1) * BS]
            return carry
        lax.fori_loop(0, count, one, 0)

    def block_of(index):
        return 2 * (index // per_block) + depth

    def out_share(index, core):
        inner = pl.ds((index % per_block) * piece, piece)
        place = out_ref.at[2 * (index // per_block) + core, 0, :, inner]
        return copy(place, place, out_s.at[index], out_r.at[index], sibling)

    def finish(index):
        block = block_of(index)
        inner = pl.ds(pl.multiple_of((index % per_block) * piece, piece), piece)
        taken = branch_ref[block] == 1
        for slot in range(slots):
            square = total[lax.rem(cols_ref[block, 0, slot], slots), some(index)]
            out_ref[block, 0, slot, inner] = jnp.where(taken, square, 2.0 * mine[index // per_block, slot, inner] - square)
        out_share(index, depth).start()

    def loop(begin, end_at, body):
        def one(index, carry):
            body(index)
            return carry
        lax.fori_loop(begin, end_at, one, 0)

    def tell(stage, target):
        pl.semaphore_signal(ready.at[stage], inc=1, device_id=target, device_id_type=MESH)

    def hear(stage):
        pl.semaphore_wait(ready.at[stage], 1)

    tell(0, plane[0])

    @pl.when(outer)
    def _():
        loop(0, PIECES, lambda i: up(i).start())
        for index in range(CHUNKS):
            for axis in range(2):
                near(axis, index).start()
        take_blocks(range(CHUNKS, panel))
        total[...] = jnp.zeros_like(total)
        split(tile, row, 0, panel)
        for index in range(CHUNKS):
            for axis in range(2):
                take_near(axis, index)
            if index == 0:
                hear(0)
                tell(1, plane[1])
            if index == 1:
                hear(1)
                tell(2, partner)

        @pl.when(mrow == 0)
        def _():
            lift().start()

        for index in range(CHUNKS):
            for axis in range(2):
                near_place(axis, index, 1 - depth)[1].wait_recv()
        for axis in range(2):
            split(right.at[beside[axis]], beside[axis], 0, panel)
        for index in range(CHUNKS):
            take_far(index)
        for index in range(CHUNKS):
            far_place(index, 1 - depth)[1].wait_recv()
        split(right.at[corner], corner, 0, panel)
        accumulate(end, 0, CHUNKS)

        def arrived(which, index):
            @pl.when(goes_down(which, index))
            def _():
                place = left.at[(mid, group1, group2)[which], some(index)]
                copy(place, place, down_s.at[which, index], down_r.at[which, index], sibling).wait_recv()

        for which in range(3):
            loop(0, PIECES, lambda i: arrived(which, i))
            if which == 1:
                accumulate(direct, 0, CHUNKS)
                accumulate(summed, 0, 1)
        accumulate(group2, 0, 1)
        loop(0, WHOLE, finish)
        hear(4)

        def last(index):
            at = some(index)
            place = partial_in.at[at]
            copy(place, place, part_s.at[index], part_r.at[index], sibling).wait_recv()
            value = partial_in[at]
            for slot in range(slots):
                total[slot, some(index + WHOLE)] += value[:, slot * BS:(slot + 1) * BS]
            finish(index + WHOLE)

        loop(0, PIECES - WHOLE, last)

    @pl.when(jnp.logical_not(outer))
    def _():
        cross(0, 0).start()
        for axis in range(2):
            near(axis, 0).start()
        loop(0, WHOLE, lambda i: down(0, i).start())

        @pl.when(mrow != 3)
        def _():
            loop(1, PIECES, lambda i: cross(0, i).start())

        @pl.when(mrow >= 2)
        def _():
            loop(WHOLE, PIECES, lambda i: down(0, i).start())

        def late_near(axis):
            for index in range(1, CHUNKS):
                near(axis, index).start()

        for axis in range(2):
            pl.when(jnp.logical_not(gives(axis, 0)))(functools.partial(late_near, axis))
        take_blocks(range(CHUNKS, panel))
        total[...] = jnp.zeros_like(total)
        split(tile, row, 0, panel)

        def first(index):
            up(index).wait_recv()
            cross(1, index).start()
            for axis in range(2):
                @pl.when(gives(axis, index))
                def _(axis=axis):
                    give(axis, index).start()

            @pl.when(mrow != 0)
            def _():
                own_share(index, depth).start()

            cross_in(False, index).wait_recv()

            @pl.when(goes_down(1, index))
            def _():
                down(1, index).start()

            @pl.when(index == 1)
            def _():
                for axis in range(2):
                    take_near(axis, 0, False)

            @pl.when(index >= 2)
            def _():
                for axis in range(2):
                    take_given(axis, index - 2)

        loop(0, PIECES, first)

        @pl.when(mrow == 3)
        def _():
            loop(1, PIECES, lambda i: cross(0, i).start())

        for axis in range(2):
            pl.when(gives(axis, 0))(functools.partial(late_near, axis))
        for axis in range(2):
            pass_far(axis, 0)
        hear(0)
        tell(1, plane[1])
        early = (mrow == 1, mrow >= 2)
        for axis in range(2):
            @pl.when(early[axis])
            def _(axis=axis):
                for index in range(1, CHUNKS):
                    take_near(axis, index)

        @pl.when(mrow != 3)
        def _():
            accumulate(row, 0, CHUNKS)

        for index in range(WHOLE):
            cross_in(True, index).wait_recv()
            down(2, index).start()
            for axis in range(2):
                take_given(axis, PIECES - 2 + index)

        @pl.when(mrow == 0)
        def _():
            place, share = lift_place(depth)
            copy(place, place, lift_s.at[0], lift_r.at[0], sibling).wait_recv()
            share.start()
            lift_place(1 - depth)[1].wait_recv()

        def shared(index):
            for axis in range(2):
                @pl.when(given(axis, index))
                def _(axis=axis):
                    give_place(axis, index, 1 - depth)[1].wait_recv()

            @pl.when(mrow != 0)
            def _():
                own_share(index, 1 - depth).wait_recv()

        loop(0, PIECES, shared)

        @pl.when(mrow != 0)
        def _():
            for index in range(CHUNKS):
                extra[own_slot, chunk(index, depth)] = left[end, index * BS:(index + 1) * BS]

        for slot in range(2):
            split(extra.at[slot], groups + slot, 0, panel)

        def begin_part(index):
            at = pl.ds(pl.multiple_of(index * BS, BS), BS)
            rows = pl.ds(pl.multiple_of(index * BS + WHOLE * piece, piece), BS)
            partial[at] = times(left[summed, rows], groups, everything)

        loop(0, partial.shape[0] // BS, begin_part)
        hear(1)

        def send_part(index):
            cross_in(True, index).wait_recv()
            at = some(index - WHOLE)
            partial[at] += times(left[group2, some(index)], groups + 1, everything)
            down_part(index - WHOLE).start()

        def take_late(index):
            for axis in range(2):
                @pl.when(jnp.logical_not(early[axis]))
                def _(axis=axis):
                    take_near(axis, index)

        loop(WHOLE, 4, send_part)
        hear(2)
        tell(3, opposite)
        take_late(1)
        loop(4, PIECES, send_part)
        hear(3)
        tell(4, partner)
        take_late(2)
        for axis in range(2):
            for index in range(CHUNKS):
                near_place(axis, index, 1 - depth)[1].wait_recv()
            split(right.at[beside[axis]], beside[axis], 0, panel)
            accumulate(beside[axis], 0, CHUNKS)

        @pl.when(mrow == 3)
        def _():
            accumulate(row, 0, CHUNKS)

        for index in range(CHUNKS):
            take_far(index)
            far_place(index, 1 - depth)[1].wait_recv()
            split(right.at[corner], corner, 2 * index, 2)
            accumulate(corner, 0, CHUNKS, pl.ds(2 * index * BS, 2 * BS))
        loop(0, PIECES, finish)

    eye = lax.broadcasted_iota(jnp.int32, (BS, BS), 0) == lax.broadcasted_iota(jnp.int32, (BS, BS), 1)
    lane = lax.broadcasted_iota(jnp.int32, parts.shape[1:], 1)

    def pair_copy():
        return copy(pair.at[0], pair.at[1], pair_s.at[0], pair_r.at[0], sibling)

    def t_copy(peer):
        return copy(parts.at[row], parts.at[row], t_send.at[peer], t_recv.at[row], (peer // groups, peer % groups, depth))

    def to_peers(act):
        def one(peer):
            @pl.when(peer != row * groups + col)
            def _():
                act(t_copy(peer))
        loop(0, groups * groups, one)

    @pl.when(row == col)
    def _():
        old_sum = jnp.zeros((BS, BS), jnp.float32)
        new_sum = jnp.zeros((BS, BS), jnp.float32)
        for index in range(CHUNKS):
            block = 2 * index + depth
            at = pl.ds(pl.multiple_of(block * BS, BS), BS)
            old = tile[at, at]
            square = total[block, index * BS:(index + 1) * BS]
            new = jnp.where(branch_ref[block] == 1, square, 2.0 * old - square)
            old_sum += jnp.where(eye, old, 0.0)
            new_sum += jnp.where(eye, new, 0.0)
        pair[0] = jnp.where(lane == 0, jnp.sum(old_sum), jnp.where(lane == 1, jnp.sum(new_sum), 0.0))
        pair_copy().start()
        pair_copy().wait_recv()
        parts[row] = pair[0] + pair[1]
        to_peers(lambda c: c.start())

    for source in range(groups):
        @pl.when(jnp.logical_or(row != source, col != source))
        def _(source=source):
            copy(parts.at[source], parts.at[source], t_send.at[source], t_recv.at[source], sibling).wait_recv()
    sum_all = parts[0]
    for source in range(1, groups):
        sum_all = sum_all + parts[source]
    trace_ref[...] = sum_all

    @pl.when(row == col)
    def _():
        pair_copy().wait_send()
        to_peers(lambda c: c.wait_send())

    for axis in range(2):
        for index in range(CHUNKS):
            near(axis, index).wait_send()
            near_place(axis, index, depth)[1].wait_send()

            @pl.when(goes_far(axis, index))
            def _(axis=axis, index=index):
                far(axis, index).wait_send()
    for index in range(CHUNKS):
        far_place(index, depth)[1].wait_send()

    @pl.when(outer)
    def _():
        loop(0, PIECES, lambda i: up(i).wait_send())

        @pl.when(mrow == 0)
        def _():
            lift().wait_send()

    @pl.when(jnp.logical_not(outer))
    def _():
        def sent(index):
            for which in range(2):
                cross(which, index).wait_send()
            for which in range(3):
                @pl.when(goes_down(which, index))
                def _(which=which):
                    down(which, index).wait_send()
            for axis in range(2):
                @pl.when(gives(axis, index))
                def _(axis=axis):
                    give(axis, index).wait_send()

                @pl.when(given(axis, index))
                def _(axis=axis):
                    give_place(axis, index, depth)[1].wait_send()

            @pl.when(mrow != 0)
            def _():
                own_share(index, depth).wait_send()

        loop(0, PIECES, sent)
        loop(0, PIECES - WHOLE, lambda i: down_part(i).wait_send())

        @pl.when(mrow == 0)
        def _():
            lift_place(depth)[1].wait_send()

    def last_share(index):
        out_share(index, 1 - depth).wait_recv()
        out_share(index, depth).wait_send()

    loop(0, PIECES, last_share)


def full_rows(groups, blocks, columns, branch):
    panel, _, slots = blocks.shape[:3]
    size = panel * BS
    half = size // 2
    later = half - WHOLE * (half // PIECES)
    sems = pltpu.SemaphoreType.DMA
    vmem = pl.BlockSpec(memory_space=pltpu.VMEM)
    smem = pl.BlockSpec(memory_space=pltpu.SMEM)

    def both(*shape):
        return [sems(shape), sems(shape)]

    updated, traces = pl.pallas_call(
        square_kernel,
        out_shape=(
            pltpu.VMEM(blocks.shape, jnp.float32),
            jax.ShapeDtypeStruct((8, BS), jnp.float32),
        ),
        in_specs=[smem, smem, pl.BlockSpec(memory_space=pl.ANY)],
        out_specs=(vmem, vmem),
        scratch_shapes=[
            pltpu.VMEM((panel // 2, slots, BS, BS), jnp.float32),
            pltpu.VMEM((panel // 2, slots, BS, BS), jnp.float32),
            pltpu.VMEM((size, size), jnp.float32),
            pltpu.VMEM((groups, half, size), jnp.float32),
            pltpu.VMEM((groups, size, size), jnp.float32),
            pltpu.VMEM((2, size, size), jnp.float32),
            pltpu.VMEM((groups + 2, size, size), jnp.bfloat16),
            pltpu.VMEM((groups + 2, size, size), jnp.bfloat16),
            pltpu.VMEM((slots, half, BS), jnp.float32),
            pltpu.VMEM((later, size), jnp.float32),
            pltpu.VMEM((later, size), jnp.float32),
            pltpu.VMEM((2, 8, BS), jnp.float32),
            pltpu.VMEM((groups, 8, BS), jnp.float32),
            sems((panel,)),
            *both(2, PIECES),
            *both(PIECES),
            *both(3, PIECES),
            *both(PIECES - WHOLE),
            *both(2, CHUNKS),
            sems((2, CHUNKS)),
            sems((CHUNKS,)),
            *both(2, PIECES),
            *both(1),
            *both(2, CHUNKS),
            *both(CHUNKS),
            *both(2, PIECES),
            *both(PIECES),
            *both(1),
            *both(PIECES),
            *both(1),
            sems((groups * groups,)),
            sems((groups,)),
            pltpu.SemaphoreType.REGULAR((5,)),
        ],
        compiler_params=pltpu.CompilerParams(
            collective_id=0, has_side_effects=True, vmem_limit_bytes=60 * 2**20
        ),
    )(columns, branch, blocks)
    return updated, traces[0, :2]


def solution(mesh):
    placed = (P("row", "col", None, None, None), P("row", "col", None), P("row"))
    grid = mesh.shape["row"], mesh.shape["col"], mesh.shape["depth"]

    def per_device(blocks, columns, branch):
        panel, _, slots = blocks.shape[:3]
        if grid[0] == 4 and grid[1] == 4 and grid[2] == 2 and panel == slots == 2 * CHUNKS:
            return full_rows(grid[1], blocks, columns, branch)
        return on_device(blocks, columns, branch)

    return jax.shard_map(
        per_device,
        mesh=mesh,
        in_specs=placed,
        out_specs=(P("row", "col", None, None, None), P()),
        check_vma=False,
    )
```

```python
import functools

import jax
import jax.numpy as jnp
from jax import lax
from jax.experimental import pallas as pl
from jax.experimental.pallas import tpu as pltpu
from jax.sharding import PartitionSpec as P

BS = 128
SPG = 6


EXACT = lax.Precision.HIGHEST


def shifted(value, axis, steps):
    count = lax.axis_size(axis)
    pairs = [(source, (source + steps) % count) for source in range(count)]
    return lax.ppermute(value, axis, pairs)


def cannon_sum(a_blocks, a_cols, out_cols, moving, moving_cols, offset, panel, passer):
    grid_rows = lax.axis_size("row")
    my_row = lax.axis_index("row")
    out_count = a_blocks.shape[0]
    slot_total = a_blocks.shape[1] * a_blocks.shape[2]
    a_flat = a_blocks.reshape(out_count, slot_total, BS, BS)
    a_cflat = a_cols.reshape(out_count, slot_total)
    tile_rows = moving.shape[0]
    start_sum = jnp.zeros((out_count, SPG, BS, BS), jnp.float32)

    def contribute(running, pieces, piece_cols, step_index):
        source = (my_row - step_index) % grid_rows
        wanted = source * panel + offset + jnp.arange(tile_rows, dtype=jnp.int32)
        hits = (a_cflat[:, :, None] == wanted[None, None, :]).astype(jnp.float32)
        stacked = jnp.einsum("nst,nsxy->tnxy", hits, a_flat, precision=EXACT)
        matches = (piece_cols[:, None, None, :] == out_cols[None, :, :, None]).astype(jnp.float32)

        def one_tile_row(total, items):
            left_side, right_side, pairing = items
            products = jnp.einsum("nxy,byz->nbxz", left_side, right_side, precision=EXACT)
            return (total + jnp.einsum("njb,nbxz->njxz", pairing, products, precision=EXACT), 0)

        running, unused = lax.scan(one_tile_row, running, (stacked, pieces, matches))
        return running

    def turn(step_index, carry):
        running, pieces, piece_cols = carry
        running = contribute(running, pieces, piece_cols, step_index)
        pieces, piece_cols = passer(pieces, piece_cols)
        return (running, pieces, piece_cols)

    running, pieces, piece_cols = lax.fori_loop(
        0, grid_rows - 1, turn, (start_sum, moving, moving_cols)
    )
    return contribute(running, pieces, piece_cols, grid_rows - 1)


def pass_whole(pieces, piece_cols):
    return shifted((pieces, piece_cols), "row", 1)


def on_device(blocks, columns, branch):
    panel = blocks.shape[0]
    layer_count = lax.axis_size("depth")
    layer = lax.axis_index("depth")
    my_row = lax.axis_index("row")
    rows_half = panel // layer_count
    first_row = layer * rows_half
    own_blocks = blocks[:, 0]
    own_cols = columns[:, 0]
    half_blocks = lax.dynamic_slice_in_dim(blocks, first_row, rows_half, 0)
    half_cols = lax.dynamic_slice_in_dim(columns, first_row, rows_half, 0)
    a_blocks, a_cols = (
        lax.all_gather(half_blocks, "col", axis=1, tiled=True),
        lax.all_gather(half_cols, "col", axis=1, tiled=True),
    )
    partial_sum = cannon_sum(
        a_blocks, a_cols, half_cols[:, 0], own_blocks, own_cols, 0, panel, pass_whole
    )
    product = lax.all_gather(partial_sum, "depth", axis=0, tiled=True)
    chooser = (branch == 1)[:, None, None, None]
    updated = jnp.where(chooser, product, 2.0 * own_blocks - product)
    row_ids = my_row * panel + jnp.arange(panel, dtype=jnp.int32)
    on_diag = (own_cols == row_ids[:, None]).astype(jnp.float32)
    old_term = jnp.sum(on_diag * jnp.trace(own_blocks, axis1=2, axis2=3))
    new_term = jnp.sum(on_diag * jnp.trace(updated, axis1=2, axis2=3))
    traces = lax.psum(jnp.stack([old_term, new_term]), ("row", "col"))
    return (updated[:, None], traces)


MESH = pl.DeviceIdType.MESH
PIECES = 6
WHOLE = 2
CHUNKS = 3


def halves(value):
    high = value.astype(jnp.bfloat16)
    return high, (value - high.astype(jnp.float32)).astype(jnp.bfloat16)


def square_kernel(
    cols_ref, branch_ref, blocks_hbm, out_ref, trace_ref,
    mine, others, tile, left, right, extra, high_ref, low_ref, total, partial, partial_in, pair, hint, hint_in, parts,
    in_sem, cross_s, cross_r, up_s, up_r, down_s, down_r, part_s, part_r,
    near_s, near_r, far_s, far_r, give_s, give_r, lift_s, lift_r,
    near_ss, near_sr, far_ss, far_sr, give_ss, give_sr, own_ss, own_sr, lift_ss, lift_sr,
    out_s, out_r, hint_s, hint_r, pair_s, pair_r, t_send, t_recv, ready,
):
    row, col, depth = lax.axis_index("row"), lax.axis_index("col"), lax.axis_index("depth")
    panel, slots = 2 * mine.shape[0], mine.shape[1]
    groups = parts.shape[0]
    size = tile.shape[0]
    half = size // 2
    piece = half // PIECES
    per_block = BS // piece
    side = col // 2

    def mirrored(value):
        return value + side * (3 - 2 * value)

    mrow, mcol = mirrored(row), mirrored(col)
    outer = mcol == 0
    end, mid, mid2, end2 = mirrored(0), mirrored(1), mirrored(2), mirrored(3)
    group1 = jnp.where(mrow == 0, end2, mid2)
    group2 = jnp.where(mrow == 0, mid2, end2)
    direct = jnp.where(mrow < 2, group1, mid)
    summed = jnp.where(mrow < 2, mid, group1)
    x_row, y_row, corner = row + 1 - 2 * (row % 2), (row + 2) % 4, 3 - row
    mrow_x, mrow_y = mrow + 1 - 2 * (mrow % 2), (mrow + 2) % 4
    beside = (x_row, y_row)
    sibling = (row, col, 1 - depth)
    plane = ((x_row, col, depth), (y_row, col, depth))
    partner = (row, col + 1 - 2 * (col % 2), depth)
    opposite = (row, 3 - col, depth)

    barrier = pltpu.get_barrier_semaphore()
    for peer in (sibling,) + plane + (partner,):
        pl.semaphore_signal(barrier, inc=1, device_id=peer, device_id_type=MESH)

    @pl.when(jnp.logical_not(outer))
    def _():
        pl.semaphore_signal(barrier, inc=1, device_id=opposite, device_id_type=MESH)

    def incoming(turn):
        block = 2 * (turn % CHUNKS) + (depth + turn // CHUNKS) % 2
        place = mine if turn < CHUNKS else others
        return block, pltpu.make_async_copy(blocks_hbm.at[block, 0], place.at[turn % CHUNKS], in_sem.at[turn])

    def ordered(turn):
        block = incoming(turn)[0]
        place = mine if turn < CHUNKS else others
        at = pl.ds(pl.multiple_of(block * BS, BS), BS)
        for target_slot in range(slots):
            source = 0
            for slot in range(1, slots):
                source = jnp.where(lax.rem(cols_ref[block, 0, slot], slots) == target_slot, slot, source)
            value = place[turn % CHUNKS, source]
            tile[at, target_slot * BS:(target_slot + 1) * BS] = value
            if turn < CHUNKS:
                left[col, turn * BS:(turn + 1) * BS, target_slot * BS:(target_slot + 1) * BS] = value

    def take_blocks(turns):
        for turn in turns:
            incoming(turn)[1].wait()
        for turn in turns:
            ordered(turn)

    for turn in range(panel):
        incoming(turn)[1].start()
    take_blocks(range(CHUNKS))
    pl.semaphore_wait(barrier, jnp.where(outer, 4, 5))

    def copy(src, dst, send, recv, target):
        return pltpu.make_async_remote_copy(
            src_ref=src, dst_ref=dst, send_sem=send, recv_sem=recv, device_id=target, device_id_type=MESH
        )

    def some(index, count=1):
        return pl.ds(pl.multiple_of(index * piece, piece), count * piece)

    def spot(index, core):
        start = (2 * (index // per_block) + core) * BS + (index % per_block) * piece
        return pl.ds(pl.multiple_of(start, piece), piece)

    def chunk(index, core):
        return pl.ds(pl.multiple_of((2 * index + core) * BS, BS), BS)

    def cross(which, index):
        place = left.at[col if which == 0 else end, some(index)]
        return copy(place, place, cross_s.at[which, index], cross_r.at[which, index], opposite)

    def cross_in(second, index):
        which = jnp.where((mrow == 0) != second, 1, 0)
        place = left.at[group2 if second else group1, some(index)]
        return copy(place, place, cross_s.at[which, index], cross_r.at[which, index], sibling)

    def up(index):
        place = left.at[end, some(index)]
        return copy(place, place, up_s.at[index], up_r.at[index], partner)

    def down(which, index):
        place = left.at[(mid, group1, group2)[which], some(index)]
        return copy(place, place, down_s.at[which, index], down_r.at[which, index], partner)

    def goes_down(which, index):
        whole = index < WHOLE
        if which == 2:
            return whole
        return jnp.logical_or(whole, mrow >= 2 if which == 0 else mrow < 2)

    def down_part(index):
        at = some(index)
        return copy(partial.at[at], partial_in.at[at], part_s.at[index], part_r.at[index], partner)

    def near(axis, index):
        at = chunk(index, depth)
        return copy(tile.at[at], right.at[row, at], near_s.at[axis, index], near_r.at[axis, index], plane[axis])

    def near_place(axis, index, core):
        place = right.at[beside[axis], chunk(index, core)]
        return place, copy(place, place, near_ss.at[axis, index], near_sr.at[axis, index], sibling)

    def far(axis, index):
        place = right.at[beside[1 - axis], spot(index, depth)]
        return copy(place, place, far_s.at[axis, index], far_r.at[index], plane[axis])

    def goes_far(axis, index):
        who = (mrow_x, mrow_y)[axis]
        turn, part = index // per_block, index % per_block
        by_x = turn == 0 or (turn == CHUNKS - 1 and part == 0)
        mixed = jnp.logical_or(outer, who == 0)
        if by_x == (axis == 0):
            return jnp.logical_or(mixed, who == 1 if axis == 0 else who >= 2)
        return jnp.logical_and(jnp.logical_not(mixed), who == 1 if axis == 0 else who >= 2)

    def far_place(index, core):
        place = right.at[corner, spot(index, core)]
        return place, copy(place, place, far_ss.at[index], far_sr.at[index], sibling)

    def parts_of(turn):
        return range(per_block * turn, per_block * (turn + 1))

    def take_near(axis, index, forward=True):
        place, share = near_place(axis, index, depth)
        copy(place, place, near_s.at[axis, index], near_r.at[axis, index], sibling).wait_recv()
        share.start()
        if forward:
            pass_far(1 - axis, index)

    def pass_far(axis, turn):
        for index in parts_of(turn):
            @pl.when(goes_far(axis, index))
            def _(index=index):
                far(axis, index).start()

    def take_far(turn):
        for index in parts_of(turn):
            place, share = far_place(index, depth)
            copy(place, place, far_s.at[0, index], far_r.at[index], sibling).wait_recv()
            share.start()

    def far_shared(turn):
        for index in parts_of(turn):
            far_place(index, 1 - depth)[1].wait_recv()

    x_slot = jnp.where(mrow == 2, 1, 0)
    x_slot_there = jnp.where(mrow_x == 2, 1, 0)
    own_slot = jnp.where(mrow == 3, 1, 0)

    def give(axis, index):
        slot = x_slot_there if axis == 0 else 1
        return copy(
            left.at[end, some(index)], extra.at[slot, spot(index, depth)],
            give_s.at[axis, index], give_r.at[axis, index], plane[axis],
        )

    def lifted(who):
        return jnp.where(who == 0, 1, CHUNKS - 1)

    gives_at_all = (mrow != 0, mrow >= 2)
    given_at_all = (mrow != 1, mrow < 2)

    def gives(axis, index):
        return jnp.logical_and(gives_at_all[axis], index // per_block != lifted((mrow_x, mrow_y)[axis]))

    def given(axis, index):
        return jnp.logical_and(given_at_all[axis], index // per_block != lifted(mrow))

    def give_place(axis, index, core):
        place = extra.at[x_slot if axis == 0 else 1, spot(index, core)]
        return place, copy(place, place, give_ss.at[axis, index], give_sr.at[axis, index], sibling)

    def take_given(axis, index):
        @pl.when(given(axis, index))
        def _():
            place, share = give_place(axis, index, depth)
            copy(place, place, give_s.at[axis, index], give_r.at[axis, index], sibling).wait_recv()
            share.start()

    def own_share(index, core):
        return copy(
            left.at[end, some(index)], extra.at[own_slot, spot(index, core)],
            own_ss.at[index], own_sr.at[index], sibling,
        )

    def lift(axis):
        at = chunk(lifted(mrow), depth)
        place = extra.at[x_slot if axis == 0 else 1, at]
        return copy(right.at[beside[axis], at], place, lift_s.at[axis], lift_r.at[axis], partner)

    def lift_place(axis, core):
        place = extra.at[x_slot if axis == 0 else 1, chunk(lifted(mrow), core)]
        return place, copy(place, place, lift_ss.at[axis], lift_sr.at[axis], sibling)

    def lifts(act):
        for axis in range(2):
            @pl.when(given_at_all[axis])
            def _(axis=axis):
                act(axis)

    def split(source, slot, begin, count):
        def one(part, carry):
            at = pl.ds(pl.multiple_of((begin + part) * BS, BS), BS)
            high_ref[slot, at], low_ref[slot, at] = halves(source[at])
            return carry
        lax.fori_loop(0, count, one, 0)

    dot = functools.partial(jnp.dot, preferred_element_type=jnp.float32)

    def times(value, slot, at):
        high, low = halves(value)
        return (dot(high, low_ref[slot, at]) + dot(low, high_ref[slot, at])) + dot(high, high_ref[slot, at])

    everything = pl.ds(0, size)

    def accumulate(group, begin, count, at=everything):
        def one(part, carry):
            rows = pl.ds(pl.multiple_of((begin + part) * BS, BS), BS)
            result = times(left[group, rows, at], group, at)
            for slot in range(slots):
                total[slot, rows] += result[:, slot * BS:(slot + 1) * BS]
            return carry
        lax.fori_loop(0, count, one, 0)

    def block_of(index):
        return 2 * (index // per_block) + depth

    def out_share(index, core):
        inner = pl.ds((index % per_block) * piece, piece)
        place = out_ref.at[2 * (index // per_block) + core, 0, :, inner]
        return copy(place, place, out_s.at[index], out_r.at[index], sibling)

    def finish(index):
        block = block_of(index)
        inner = pl.ds(pl.multiple_of((index % per_block) * piece, piece), piece)
        taken = branch_ref[block] == 1
        for slot in range(slots):
            square = total[lax.rem(cols_ref[block, 0, slot], slots), some(index)]
            out_ref[block, 0, slot, inner] = jnp.where(taken, square, 2.0 * mine[index // per_block, slot, inner] - square)
        out_share(index, depth).start()

    eye = lax.broadcasted_iota(jnp.int32, (BS, BS), 0) == lax.broadcasted_iota(jnp.int32, (BS, BS), 1)
    lane = lax.broadcasted_iota(jnp.int32, parts.shape[1:], 1)

    def old_and_new(old_sum, new_sum):
        old_all = jnp.sum(jnp.where(eye, old_sum, 0.0))
        new_all = jnp.sum(jnp.where(eye, new_sum, 0.0))
        return jnp.where(lane == 0, old_all, jnp.where(lane == 1, new_all, 0.0))

    def block_traces():
        old_sum = jnp.zeros((BS, BS), jnp.float32)
        new_sum = jnp.zeros((BS, BS), jnp.float32)
        for index in range(CHUNKS):
            block = 2 * index + depth
            at = pl.ds(pl.multiple_of(block * BS, BS), BS)
            old = tile[at, at]
            square = total[block, index * BS:(index + 1) * BS]
            new_sum += jnp.where(branch_ref[block] == 1, square, 2.0 * old - square)
            old_sum += old
        return old_and_new(old_sum, new_sum)

    def partial_traces():
        new_sum = jnp.zeros((BS, BS), jnp.float32)
        for index in range(WHOLE // per_block, CHUNKS):
            block = 2 * index + depth
            start = index * BS - WHOLE * piece
            square = partial[start:start + BS, pl.ds(pl.multiple_of(block * BS, BS), BS)]
            new_sum += jnp.where(branch_ref[block] == 1, square, -square)
        return old_and_new(jnp.zeros((BS, BS), jnp.float32), new_sum)

    def hint_copy():
        return copy(hint, hint_in, hint_s.at[0], hint_r.at[0], partner)

    def pair_copy():
        return copy(pair.at[0], pair.at[1], pair_s.at[0], pair_r.at[0], sibling)

    def t_copy(peer):
        return copy(parts.at[row], parts.at[row], t_send.at[peer], t_recv.at[row], (peer // groups, peer % groups, depth))

    def to_peers(act):
        def one(peer):
            @pl.when(peer != row * groups + col)
            def _():
                act(t_copy(peer))
        loop(0, groups * groups, one)

    def send_traces():
        pair_copy().wait_recv()
        parts[row] = pair[0] + pair[1]
        to_peers(lambda c: c.start())

    def loop(begin, end_at, body):
        def one(index, carry):
            body(index)
            return carry
        lax.fori_loop(begin, end_at, one, 0)

    def tell(stage, target):
        pl.semaphore_signal(ready.at[stage], inc=1, device_id=target, device_id_type=MESH)

    def hear(stage):
        pl.semaphore_wait(ready.at[stage], 1)

    tell(0, plane[0])

    def near_ready(axis, begin, end_at):
        for index in range(begin, end_at):
            near_place(axis, index, 1 - depth)[1].wait_recv()
        split(right.at[beside[axis]], beside[axis], 2 * begin, 2 * (end_at - begin))

    def near_part(axis, begin, end_at):
        near_ready(axis, begin, end_at)
        accumulate(beside[axis], 0, CHUNKS, pl.ds(2 * begin * BS, 2 * (end_at - begin) * BS))

    @pl.when(outer)
    def _():
        late_up = PIECES - per_block
        loop(0, late_up, lambda i: up(i).start())

        def rest_up():
            loop(late_up, PIECES, lambda i: up(i).start())

        pl.when(mrow != 0)(rest_up)
        for index in range(CHUNKS):
            for axis in range(2):
                near(axis, index).start()
        take_blocks(range(CHUNKS, panel))
        total[...] = jnp.zeros_like(total)
        split(tile, row, 0, panel)
        for index in range(CHUNKS):
            for axis in range(2):
                take_near(axis, index)
            if index == 0:
                hear(0)
                tell(1, plane[1])
            if index == 1:
                @pl.when(mrow == 0)
                def _():
                    lifts(lambda axis: lift(axis).start())
                    rest_up()

                hear(1)
                tell(2, partner)

        @pl.when(mrow != 0)
        def _():
            lifts(lambda axis: lift(axis).start())

        for index in range(CHUNKS):
            for axis in range(2):
                near_place(axis, index, 1 - depth)[1].wait_recv()
        for axis in range(2):
            split(right.at[beside[axis]], beside[axis], 0, panel)
        for index in range(CHUNKS):
            take_far(index)
        for index in range(CHUNKS):
            far_shared(index)
        split(right.at[corner], corner, 0, panel)
        accumulate(end, 0, CHUNKS)

        def arrived(which, index):
            @pl.when(goes_down(which, index))
            def _():
                place = left.at[(mid, group1, group2)[which], some(index)]
                copy(place, place, down_s.at[which, index], down_r.at[which, index], sibling).wait_recv()

        for which in range(3):
            loop(0, PIECES, lambda i: arrived(which, i))
            if which == 1:
                accumulate(direct, 0, CHUNKS)
                accumulate(summed, 0, 1)
        accumulate(group2, 0, 1)
        loop(0, WHOLE, finish)

        @pl.when(mrow == 0)
        def _():
            pair[0] = block_traces()

        hear(4)

        def last(index):
            at = some(index)
            place = partial_in.at[at]
            copy(place, place, part_s.at[index], part_r.at[index], sibling).wait_recv()
            value = partial_in[at]
            for slot in range(slots):
                total[slot, some(index + WHOLE)] += value[:, slot * BS:(slot + 1) * BS]
            finish(index + WHOLE)

        loop(0, PIECES - WHOLE - 1, last)

        @pl.when(mrow == 0)
        def _():
            copy(hint, hint_in, hint_s.at[0], hint_r.at[0], sibling).wait_recv()
            pair[0] = pair[0] + hint_in[...]
            pair_copy().start()
            send_traces()

        last(PIECES - WHOLE - 1)

    @pl.when(jnp.logical_not(outer))
    def _():
        loop(0, WHOLE, lambda i: cross(0, i).start())
        for axis in range(2):
            near(axis, 0).start()
        loop(0, WHOLE, lambda i: down(0, i).start())

        @pl.when(mrow != 3)
        def _():
            loop(WHOLE, PIECES, lambda i: cross(0, i).start())

        @pl.when(mrow >= 2)
        def _():
            loop(WHOLE, PIECES, lambda i: down(0, i).start())

        for axis in range(2):
            @pl.when(jnp.logical_not(gives_at_all[axis]))
            def _(axis=axis):
                for index in range(1, CHUNKS):
                    near(axis, index).start()

        take_blocks(range(CHUNKS, panel))
        total[...] = jnp.zeros_like(total)
        split(tile, row, 0, panel)

        mrow_there = (mrow_x, mrow_y)

        def pass_up(index):
            up(index).wait_recv()
            cross(1, index).start()

        def first(index):
            @pl.when(jnp.logical_or(mrow != 0, index < PIECES - per_block))
            def _():
                pass_up(index)

            for axis in range(2):
                @pl.when(gives(axis, index))
                def _(axis=axis):
                    give(axis, index).start()

                for turn in range(1, CHUNKS):
                    moment = jnp.where(mrow_there[axis] == 0, (1, 5)[turn - 1], 3)

                    @pl.when(jnp.logical_and(gives_at_all[axis], index == moment))
                    def _(axis=axis, turn=turn):
                        near(axis, turn).start()

            @pl.when(mrow != 0)
            def _():
                own_share(index, depth).start()

            cross_in(False, index).wait_recv()

            @pl.when(goes_down(1, index))
            def _():
                down(1, index).start()

            @pl.when(index == 1)
            def _():
                for axis in range(2):
                    take_near(axis, 0, False)
                for axis in range(2):
                    pl.when(jnp.logical_not(gives_at_all[axis]))(functools.partial(pass_far, axis, 0))

            @pl.when(jnp.logical_and(mrow == 0, index == PIECES - 2))
            def _():
                for axis in range(2):
                    take_near(axis, 1)

            @pl.when(index >= 2)
            def _():
                for axis in range(2):
                    take_given(axis, index - 2)

        def whole_group2(index):
            cross_in(True, index).wait_recv()
            down(2, index).start()

        pl.when(mrow == 0)(lambda: loop(0, WHOLE, whole_group2))
        loop(0, PIECES, first)

        @pl.when(mrow == 3)
        def _():
            loop(WHOLE, PIECES, lambda i: cross(0, i).start())

        for axis in range(2):
            pl.when(gives_at_all[axis])(functools.partial(pass_far, axis, 0))
        hear(0)
        tell(1, plane[1])
        early = (mrow == 1, mrow >= 2)
        for axis in range(2):
            @pl.when(early[axis])
            def _(axis=axis):
                for turn in range(1, CHUNKS):
                    take_near(axis, turn)

        @pl.when(mrow == 0)
        def _():
            near_part(0, 0, 2)

        @pl.when(jnp.logical_or(mrow == 1, mrow == 2))
        def _():
            accumulate(row, 0, CHUNKS)

        @pl.when(mrow == 3)
        def _():
            near_part(1, 0, CHUNKS)

        for index in range(WHOLE):
            pl.when(mrow != 0)(functools.partial(whole_group2, index))
            for axis in range(2):
                take_given(axis, PIECES - 2 + index)

        def take_lift(axis):
            place, share = lift_place(axis, depth)
            copy(place, place, lift_s.at[axis], lift_r.at[axis], sibling).wait_recv()
            share.start()

        lifts(take_lift)
        lifts(lambda axis: lift_place(axis, 1 - depth)[1].wait_recv())

        def shared(index):
            for axis in range(2):
                @pl.when(given(axis, index))
                def _(axis=axis):
                    give_place(axis, index, 1 - depth)[1].wait_recv()

            @pl.when(mrow != 0)
            def _():
                own_share(index, 1 - depth).wait_recv()

        loop(0, PIECES, shared)

        @pl.when(mrow != 0)
        def _():
            for index in range(CHUNKS):
                extra[own_slot, chunk(index, depth)] = left[end, index * BS:(index + 1) * BS]

        for slot in range(2):
            split(extra.at[slot], groups + slot, 0, panel)

        def begin_part(index):
            at = pl.ds(pl.multiple_of(index * BS, BS), BS)
            rows = pl.ds(pl.multiple_of(index * BS + WHOLE * piece, piece), BS)
            partial[at] = times(left[summed, rows], groups, everything)

        loop(0, partial.shape[0] // BS, begin_part)
        hear(1)

        def send_part(index):
            cross_in(True, index).wait_recv()
            at = some(index - WHOLE)
            partial[at] += times(left[group2, some(index)], groups + 1, everything)

            @pl.when(jnp.logical_and(mrow == 0, index == PIECES - 1))
            def _():
                hint[...] = partial_traces()
                hint_copy().start()

            down_part(index - WHOLE).start()

        def corner_part(turn):
            take_far(turn)
            far_shared(turn)
            split(right.at[corner], corner, 2 * turn, 2)
            if turn < CHUNKS - 1:
                accumulate(corner, 0, CHUNKS, pl.ds(2 * turn * BS, 2 * BS))

        send_part(WHOLE)
        pl.when(mrow == 0)(lambda: pass_up(PIECES - 2))
        for axis in range(2):
            @pl.when(jnp.logical_and(mrow != 0, jnp.logical_not(early[axis])))
            def _(axis=axis):
                take_near(axis, 1)

        @pl.when(mrow == 1)
        def _():
            near_part(0, 0, CHUNKS)

        @pl.when(mrow == 2)
        def _():
            near_part(1, 0, CHUNKS)

        @pl.when(mrow == 3)
        def _():
            near_part(0, 0, 2)

        hear(2)
        tell(3, opposite)
        send_part(WHOLE + 1)
        pl.when(mrow == 0)(lambda: pass_up(PIECES - 1))
        for axis in range(2):
            @pl.when(jnp.logical_not(early[axis]))
            def _(axis=axis):
                take_near(axis, 2)

        @pl.when(mrow == 0)
        def _():
            accumulate(row, 0, CHUNKS)

        @pl.when(mrow == 3)
        def _():
            near_part(0, 2, CHUNKS)

        @pl.when(mrow != 0)
        def _():
            corner_part(0)

        send_part(WHOLE + 2)

        @pl.when(mrow < 2)
        def _():
            near_ready(1, 0, CHUNKS)

        @pl.when(mrow == 2)
        def _():
            near_ready(0, 0, CHUNKS)

        accumulate(group2, 0, 2)

        @pl.when(mrow != 0)
        def _():
            corner_part(1)

        send_part(WHOLE + 3)
        hear(3)
        tell(4, partner)
        accumulate(group2, 2, 1)

        @pl.when(mrow == 0)
        def _():
            near_part(0, 2, CHUNKS)
            corner_part(0)
            corner_part(1)

        corner_part(2)
        at = pl.ds(2 * (CHUNKS - 1) * BS, 2 * BS)

        def last_block(index):
            accumulate(corner, index, 1, at)
            loop(per_block * index, per_block * (index + 1), finish)

        pl.when(mrow != 1)(lambda: loop(0, CHUNKS, last_block))

        @pl.when(mrow == 1)
        def _():
            accumulate(corner, 0, CHUNKS, at)
            pair[0] = block_traces()
            pair_copy().start()
            loop(0, PIECES, finish)
            send_traces()


    for source in range(groups):
        @pl.when(jnp.logical_or(row != source, col != source))
        def _(source=source):
            copy(parts.at[source], parts.at[source], t_send.at[source], t_recv.at[source], sibling).wait_recv()
    sum_all = parts[0]
    for source in range(1, groups):
        sum_all = sum_all + parts[source]
    first_row = lax.broadcasted_iota(jnp.int32, parts.shape[1:], 0) == 0
    for index in range(2):
        trace_ref[index] = jnp.sum(jnp.where(jnp.logical_and(first_row, lane == index), sum_all, 0.0))

    @pl.when(row == col)
    def _():
        pair_copy().wait_send()
        to_peers(lambda c: c.wait_send())

    for axis in range(2):
        for index in range(CHUNKS):
            near(axis, index).wait_send()
            near_place(axis, index, depth)[1].wait_send()
        for index in range(PIECES):
            @pl.when(goes_far(axis, index))
            def _(axis=axis, index=index):
                far(axis, index).wait_send()
    for index in range(PIECES):
        far_place(index, depth)[1].wait_send()

    @pl.when(outer)
    def _():
        loop(0, PIECES, lambda i: up(i).wait_send())

        lifts(lambda axis: lift(axis).wait_send())

    @pl.when(jnp.logical_not(outer))
    def _():
        def sent(index):
            for which in range(2):
                cross(which, index).wait_send()
            for which in range(3):
                @pl.when(goes_down(which, index))
                def _(which=which):
                    down(which, index).wait_send()
            for axis in range(2):
                @pl.when(gives(axis, index))
                def _(axis=axis):
                    give(axis, index).wait_send()

                @pl.when(given(axis, index))
                def _(axis=axis):
                    give_place(axis, index, depth)[1].wait_send()

            @pl.when(mrow != 0)
            def _():
                own_share(index, depth).wait_send()

        loop(0, PIECES, sent)
        loop(0, PIECES - WHOLE, lambda i: down_part(i).wait_send())
        pl.when(mrow == 0)(lambda: hint_copy().wait_send())

        lifts(lambda axis: lift_place(axis, depth)[1].wait_send())

    def last_share(index):
        out_share(index, 1 - depth).wait_recv()
        out_share(index, depth).wait_send()

    loop(0, PIECES, last_share)


def full_rows(groups, blocks, columns, branch):
    panel, _, slots = blocks.shape[:3]
    size = panel * BS
    half = size // 2
    later = half - WHOLE * (half // PIECES)
    sems = pltpu.SemaphoreType.DMA
    vmem = pl.BlockSpec(memory_space=pltpu.VMEM)
    smem = pl.BlockSpec(memory_space=pltpu.SMEM)

    def both(*shape):
        return [sems(shape), sems(shape)]

    return pl.pallas_call(
        square_kernel,
        out_shape=(
            pltpu.VMEM(blocks.shape, jnp.float32),
            jax.ShapeDtypeStruct((2,), jnp.float32),
        ),
        in_specs=[smem, smem, pl.BlockSpec(memory_space=pl.ANY)],
        out_specs=(vmem, smem),
        scratch_shapes=[
            pltpu.VMEM((panel // 2, slots, BS, BS), jnp.float32),
            pltpu.VMEM((panel // 2, slots, BS, BS), jnp.float32),
            pltpu.VMEM((size, size), jnp.float32),
            pltpu.VMEM((groups, half, size), jnp.float32),
            pltpu.VMEM((groups, size, size), jnp.float32),
            pltpu.VMEM((2, size, size), jnp.float32),
            pltpu.VMEM((groups + 2, size, size), jnp.bfloat16),
            pltpu.VMEM((groups + 2, size, size), jnp.bfloat16),
            pltpu.VMEM((slots, half, BS), jnp.float32),
            pltpu.VMEM((later, size), jnp.float32),
            pltpu.VMEM((later, size), jnp.float32),
            pltpu.VMEM((2, 8, BS), jnp.float32),
            pltpu.VMEM((8, BS), jnp.float32),
            pltpu.VMEM((8, BS), jnp.float32),
            pltpu.VMEM((groups, 8, BS), jnp.float32),
            sems((panel,)),
            *both(2, PIECES),
            *both(PIECES),
            *both(3, PIECES),
            *both(PIECES - WHOLE),
            *both(2, CHUNKS),
            sems((2, PIECES)),
            sems((PIECES,)),
            *both(2, PIECES),
            *both(2),
            *both(2, CHUNKS),
            *both(PIECES),
            *both(2, PIECES),
            *both(PIECES),
            *both(2),
            *both(PIECES),
            *both(1),
            *both(1),
            sems((groups * groups,)),
            sems((groups,)),
            pltpu.SemaphoreType.REGULAR((5,)),
        ],
        compiler_params=pltpu.CompilerParams(
            collective_id=0, has_side_effects=True, vmem_limit_bytes=60 * 2**20
        ),
    )(columns, branch, blocks)


def solution(mesh):
    placed = (P("row", "col", None, None, None), P("row", "col", None), P("row"))
    grid = mesh.shape["row"], mesh.shape["col"], mesh.shape["depth"]

    def per_device(blocks, columns, branch):
        panel, _, slots = blocks.shape[:3]
        if grid[0] == 4 and grid[1] == 4 and grid[2] == 2 and panel == slots == 2 * CHUNKS:
            return full_rows(grid[1], blocks, columns, branch)
        return on_device(blocks, columns, branch)

    return jax.shard_map(
        per_device,
        mesh=mesh,
        in_specs=placed,
        out_specs=(P("row", "col", None, None, None), P()),
        check_vma=False,
    )
```

```python
import functools

import jax
import jax.numpy as jnp
from jax import lax
from jax.experimental import pallas as pl
from jax.experimental.pallas import tpu as pltpu
from jax.sharding import PartitionSpec as P

BS = 128
SPG = 6


EXACT = lax.Precision.HIGHEST


def shifted(value, axis, steps):
    count = lax.axis_size(axis)
    pairs = [(source, (source + steps) % count) for source in range(count)]
    return lax.ppermute(value, axis, pairs)


def cannon_sum(a_blocks, a_cols, out_cols, moving, moving_cols, offset, panel, passer):
    grid_rows = lax.axis_size("row")
    my_row = lax.axis_index("row")
    out_count = a_blocks.shape[0]
    slot_total = a_blocks.shape[1] * a_blocks.shape[2]
    a_flat = a_blocks.reshape(out_count, slot_total, BS, BS)
    a_cflat = a_cols.reshape(out_count, slot_total)
    tile_rows = moving.shape[0]
    start_sum = jnp.zeros((out_count, SPG, BS, BS), jnp.float32)

    def contribute(running, pieces, piece_cols, step_index):
        source = (my_row - step_index) % grid_rows
        wanted = source * panel + offset + jnp.arange(tile_rows, dtype=jnp.int32)
        hits = (a_cflat[:, :, None] == wanted[None, None, :]).astype(jnp.float32)
        stacked = jnp.einsum("nst,nsxy->tnxy", hits, a_flat, precision=EXACT)
        matches = (piece_cols[:, None, None, :] == out_cols[None, :, :, None]).astype(jnp.float32)

        def one_tile_row(total, items):
            left_side, right_side, pairing = items
            products = jnp.einsum("nxy,byz->nbxz", left_side, right_side, precision=EXACT)
            return (total + jnp.einsum("njb,nbxz->njxz", pairing, products, precision=EXACT), 0)

        running, unused = lax.scan(one_tile_row, running, (stacked, pieces, matches))
        return running

    def turn(step_index, carry):
        running, pieces, piece_cols = carry
        running = contribute(running, pieces, piece_cols, step_index)
        pieces, piece_cols = passer(pieces, piece_cols)
        return (running, pieces, piece_cols)

    running, pieces, piece_cols = lax.fori_loop(
        0, grid_rows - 1, turn, (start_sum, moving, moving_cols)
    )
    return contribute(running, pieces, piece_cols, grid_rows - 1)


def pass_whole(pieces, piece_cols):
    return shifted((pieces, piece_cols), "row", 1)


def on_device(blocks, columns, branch):
    panel = blocks.shape[0]
    layer_count = lax.axis_size("depth")
    layer = lax.axis_index("depth")
    my_row = lax.axis_index("row")
    rows_half = panel // layer_count
    first_row = layer * rows_half
    own_blocks = blocks[:, 0]
    own_cols = columns[:, 0]
    half_blocks = lax.dynamic_slice_in_dim(blocks, first_row, rows_half, 0)
    half_cols = lax.dynamic_slice_in_dim(columns, first_row, rows_half, 0)
    a_blocks, a_cols = (
        lax.all_gather(half_blocks, "col", axis=1, tiled=True),
        lax.all_gather(half_cols, "col", axis=1, tiled=True),
    )
    partial_sum = cannon_sum(
        a_blocks, a_cols, half_cols[:, 0], own_blocks, own_cols, 0, panel, pass_whole
    )
    product = lax.all_gather(partial_sum, "depth", axis=0, tiled=True)
    chooser = (branch == 1)[:, None, None, None]
    updated = jnp.where(chooser, product, 2.0 * own_blocks - product)
    row_ids = my_row * panel + jnp.arange(panel, dtype=jnp.int32)
    on_diag = (own_cols == row_ids[:, None]).astype(jnp.float32)
    old_term = jnp.sum(on_diag * jnp.trace(own_blocks, axis1=2, axis2=3))
    new_term = jnp.sum(on_diag * jnp.trace(updated, axis1=2, axis2=3))
    traces = lax.psum(jnp.stack([old_term, new_term]), ("row", "col"))
    return (updated[:, None], traces)


MESH = pl.DeviceIdType.MESH
PIECES = 6
WHOLE = 2
CHUNKS = 3


def halves(value):
    high = value.astype(jnp.bfloat16)
    return high, (value - high.astype(jnp.float32)).astype(jnp.bfloat16)


def square_kernel(
    cols_ref, branch_ref, blocks_hbm, out_ref, trace_ref,
    mine, others, tile, left, right, extra, high_ref, low_ref, total, partial, partial_in, pair, hint, hint_in, parts,
    in_sem, cross_s, cross_r, up_s, up_r, down_s, down_r, part_s, part_r,
    near_s, near_r, far_s, far_r, give_s, give_r, lift_s, lift_r,
    near_ss, near_sr, far_ss, far_sr, give_ss, give_sr, own_ss, own_sr, lift_ss, lift_sr,
    out_s, out_r, hint_s, hint_r, pair_s, pair_r, t_send, t_recv, ready,
):
    row, col, depth = lax.axis_index("row"), lax.axis_index("col"), lax.axis_index("depth")
    panel, slots = 2 * mine.shape[0], mine.shape[1]
    groups = parts.shape[0]
    size = tile.shape[0]
    half = size // 2
    piece = half // PIECES
    per_block = BS // piece
    side = col // 2

    def mirrored(value):
        return value + side * (3 - 2 * value)

    mrow, mcol = mirrored(row), mirrored(col)
    outer = mcol == 0
    end, mid, mid2, end2 = mirrored(0), mirrored(1), mirrored(2), mirrored(3)
    group1 = jnp.where(mrow == 0, end2, mid2)
    group2 = jnp.where(mrow == 0, mid2, end2)
    direct = jnp.where(mrow < 2, group1, mid)
    summed = jnp.where(mrow < 2, mid, group1)
    x_row, y_row, corner = row + 1 - 2 * (row % 2), (row + 2) % 4, 3 - row
    mrow_x, mrow_y = mrow + 1 - 2 * (mrow % 2), (mrow + 2) % 4
    beside = (x_row, y_row)
    sibling = (row, col, 1 - depth)
    plane = ((x_row, col, depth), (y_row, col, depth))
    partner = (row, col + 1 - 2 * (col % 2), depth)
    opposite = (row, 3 - col, depth)

    barrier = pltpu.get_barrier_semaphore()
    for peer in (sibling,) + plane + (partner,):
        pl.semaphore_signal(barrier, inc=1, device_id=peer, device_id_type=MESH)

    @pl.when(jnp.logical_not(outer))
    def _():
        pl.semaphore_signal(barrier, inc=1, device_id=opposite, device_id_type=MESH)

    def incoming(turn):
        block = 2 * (turn % CHUNKS) + (depth + turn // CHUNKS) % 2
        place = mine if turn < CHUNKS else others
        return block, pltpu.make_async_copy(blocks_hbm.at[block, 0], place.at[turn % CHUNKS], in_sem.at[turn])

    def ordered(turn):
        block = incoming(turn)[0]
        place = mine if turn < CHUNKS else others
        at = pl.ds(pl.multiple_of(block * BS, BS), BS)
        for target_slot in range(slots):
            source = 0
            for slot in range(1, slots):
                source = jnp.where(lax.rem(cols_ref[block, 0, slot], slots) == target_slot, slot, source)
            value = place[turn % CHUNKS, source]
            tile[at, target_slot * BS:(target_slot + 1) * BS] = value
            if turn < CHUNKS:
                left[col, turn * BS:(turn + 1) * BS, target_slot * BS:(target_slot + 1) * BS] = value

    def take_blocks(turns):
        for turn in turns:
            incoming(turn)[1].wait()
        for turn in turns:
            ordered(turn)

    for turn in range(CHUNKS):
        incoming(turn)[1].start()
    for turn in range(CHUNKS):
        incoming(turn)[1].wait()
    for turn in range(CHUNKS, panel):
        incoming(turn)[1].start()
    ordered(0)
    pl.semaphore_wait(barrier, jnp.where(outer, 4, 5))

    def copy(src, dst, send, recv, target):
        return pltpu.make_async_remote_copy(
            src_ref=src, dst_ref=dst, send_sem=send, recv_sem=recv, device_id=target, device_id_type=MESH
        )

    def some(index, count=1):
        return pl.ds(pl.multiple_of(index * piece, piece), count * piece)

    def spot(index, core):
        start = (2 * (index // per_block) + core) * BS + (index % per_block) * piece
        return pl.ds(pl.multiple_of(start, piece), piece)

    def chunk(index, core):
        return pl.ds(pl.multiple_of((2 * index + core) * BS, BS), BS)

    def cross(which, index):
        place = left.at[col if which == 0 else end, some(index)]
        return copy(place, place, cross_s.at[which, index], cross_r.at[which, index], opposite)

    def cross_in(second, index):
        which = jnp.where((mrow == 0) != second, 1, 0)
        place = left.at[group2 if second else group1, some(index)]
        return copy(place, place, cross_s.at[which, index], cross_r.at[which, index], sibling)

    def up(index):
        place = left.at[end, some(index)]
        return copy(place, place, up_s.at[index], up_r.at[index], partner)

    def down(which, index):
        place = left.at[(mid, group1, group2)[which], some(index)]
        return copy(place, place, down_s.at[which, index], down_r.at[which, index], partner)

    def goes_down(which, index):
        whole = index < WHOLE
        if which == 2:
            return whole
        return jnp.logical_or(whole, mrow >= 2 if which == 0 else mrow < 2)

    def down_part(index):
        at = some(index)
        return copy(partial.at[at], partial_in.at[at], part_s.at[index], part_r.at[index], partner)

    def near(axis, index):
        at = chunk(index, depth)
        return copy(tile.at[at], right.at[row, at], near_s.at[axis, index], near_r.at[axis, index], plane[axis])

    def near_place(axis, index, core):
        place = right.at[beside[axis], chunk(index, core)]
        return place, copy(place, place, near_ss.at[axis, index], near_sr.at[axis, index], sibling)

    def far(axis, index):
        place = right.at[beside[1 - axis], spot(index, depth)]
        return copy(place, place, far_s.at[axis, index], far_r.at[index], plane[axis])

    def goes_far(axis, index):
        who = (mrow_x, mrow_y)[axis]
        turn, part = index // per_block, index % per_block
        by_x = turn == 0 or (turn == CHUNKS - 1 and part == 0)
        mixed = jnp.logical_or(outer, who == 0)
        if by_x == (axis == 0):
            return jnp.logical_or(mixed, who == 1 if axis == 0 else who >= 2)
        return jnp.logical_and(jnp.logical_not(mixed), who == 1 if axis == 0 else who >= 2)

    def far_place(index, core):
        place = right.at[corner, spot(index, core)]
        return place, copy(place, place, far_ss.at[index], far_sr.at[index], sibling)

    def parts_of(turn):
        return range(per_block * turn, per_block * (turn + 1))

    def take_near(axis, index, forward=True):
        place, share = near_place(axis, index, depth)
        copy(place, place, near_s.at[axis, index], near_r.at[axis, index], sibling).wait_recv()
        share.start()
        if forward:
            pass_far(1 - axis, index)

    def pass_far(axis, turn):
        for index in parts_of(turn):
            @pl.when(goes_far(axis, index))
            def _(index=index):
                far(axis, index).start()

    def take_far(turn):
        for index in parts_of(turn):
            place, share = far_place(index, depth)
            copy(place, place, far_s.at[0, index], far_r.at[index], sibling).wait_recv()
            share.start()

    def far_shared(turn):
        for index in parts_of(turn):
            far_place(index, 1 - depth)[1].wait_recv()

    x_slot = jnp.where(mrow == 2, 1, 0)
    x_slot_there = jnp.where(mrow_x == 2, 1, 0)
    own_slot = jnp.where(mrow == 3, 1, 0)

    def give(axis, index):
        slot = x_slot_there if axis == 0 else 1
        return copy(
            left.at[end, some(index)], extra.at[slot, spot(index, depth)],
            give_s.at[axis, index], give_r.at[axis, index], plane[axis],
        )

    def lifted(who):
        return jnp.where(who == 0, 1, CHUNKS - 1)

    gives_at_all = (mrow != 0, mrow >= 2)
    given_at_all = (mrow != 1, mrow < 2)

    def gives(axis, index):
        return jnp.logical_and(gives_at_all[axis], index // per_block != lifted((mrow_x, mrow_y)[axis]))

    def given(axis, index):
        return jnp.logical_and(given_at_all[axis], index // per_block != lifted(mrow))

    def give_place(axis, index, core):
        place = extra.at[x_slot if axis == 0 else 1, spot(index, core)]
        return place, copy(place, place, give_ss.at[axis, index], give_sr.at[axis, index], sibling)

    def take_given(axis, index):
        @pl.when(given(axis, index))
        def _():
            place, share = give_place(axis, index, depth)
            copy(place, place, give_s.at[axis, index], give_r.at[axis, index], sibling).wait_recv()
            share.start()

    def own_share(index, core):
        return copy(
            left.at[end, some(index)], extra.at[own_slot, spot(index, core)],
            own_ss.at[index], own_sr.at[index], sibling,
        )

    def lift(axis):
        at = chunk(lifted(mrow), depth)
        place = extra.at[x_slot if axis == 0 else 1, at]
        return copy(right.at[beside[axis], at], place, lift_s.at[axis], lift_r.at[axis], partner)

    def lift_place(axis, core):
        place = extra.at[x_slot if axis == 0 else 1, chunk(lifted(mrow), core)]
        return place, copy(place, place, lift_ss.at[axis], lift_sr.at[axis], sibling)

    def lifts(act):
        for axis in range(2):
            @pl.when(given_at_all[axis])
            def _(axis=axis):
                act(axis)

    def split(source, slot, begin, count):
        def one(part, carry):
            at = pl.ds(pl.multiple_of((begin + part) * BS, BS), BS)
            high_ref[slot, at], low_ref[slot, at] = halves(source[at])
            return carry
        lax.fori_loop(0, count, one, 0)

    dot = functools.partial(jnp.dot, preferred_element_type=jnp.float32)

    def times(value, slot, at):
        high, low = halves(value)
        return (dot(high, low_ref[slot, at]) + dot(low, high_ref[slot, at])) + dot(high, high_ref[slot, at])

    everything = pl.ds(0, size)

    def accumulate(group, begin, count, at=everything):
        if count == CHUNKS:
            result = times(left[group, :, at], group, at)
            for slot in range(slots):
                total[slot] += result[:, slot * BS:(slot + 1) * BS]
            return

        def one(part, carry):
            rows = pl.ds(pl.multiple_of((begin + part) * BS, BS), BS)
            result = times(left[group, rows, at], group, at)
            for slot in range(slots):
                total[slot, rows] += result[:, slot * BS:(slot + 1) * BS]
            return carry
        lax.fori_loop(0, count, one, 0)

    def block_of(index):
        return 2 * (index // per_block) + depth

    def out_share(index, core):
        inner = pl.ds((index % per_block) * piece, piece)
        place = out_ref.at[2 * (index // per_block) + core, 0, :, inner]
        return copy(place, place, out_s.at[index], out_r.at[index], sibling)

    def finish(index):
        block = block_of(index)
        inner = pl.ds(pl.multiple_of((index % per_block) * piece, piece), piece)
        taken = branch_ref[block] == 1
        for slot in range(slots):
            square = total[lax.rem(cols_ref[block, 0, slot], slots), some(index)]
            out_ref[block, 0, slot, inner] = jnp.where(taken, square, 2.0 * mine[index // per_block, slot, inner] - square)
        out_share(index, depth).start()

    eye = lax.broadcasted_iota(jnp.int32, (BS, BS), 0) == lax.broadcasted_iota(jnp.int32, (BS, BS), 1)
    lane = lax.broadcasted_iota(jnp.int32, parts.shape[1:], 1)

    def old_and_new(old_sum, new_sum):
        old_all = jnp.sum(jnp.where(eye, old_sum, 0.0))
        new_all = jnp.sum(jnp.where(eye, new_sum, 0.0))
        return jnp.where(lane == 0, old_all, jnp.where(lane == 1, new_all, 0.0))

    def block_traces():
        old_sum = jnp.zeros((BS, BS), jnp.float32)
        new_sum = jnp.zeros((BS, BS), jnp.float32)
        for index in range(CHUNKS):
            block = 2 * index + depth
            at = pl.ds(pl.multiple_of(block * BS, BS), BS)
            old = tile[at, at]
            square = total[block, index * BS:(index + 1) * BS]
            new_sum += jnp.where(branch_ref[block] == 1, square, 2.0 * old - square)
            old_sum += old
        return old_and_new(old_sum, new_sum)

    def partial_traces():
        new_sum = jnp.zeros((BS, BS), jnp.float32)
        for index in range(WHOLE // per_block, CHUNKS):
            block = 2 * index + depth
            start = index * BS - WHOLE * piece
            square = partial[start:start + BS, pl.ds(pl.multiple_of(block * BS, BS), BS)]
            new_sum += jnp.where(branch_ref[block] == 1, square, -square)
        return old_and_new(jnp.zeros((BS, BS), jnp.float32), new_sum)

    def hint_copy():
        return copy(hint, hint_in, hint_s.at[0], hint_r.at[0], partner)

    def pair_copy():
        return copy(pair.at[0], pair.at[1], pair_s.at[0], pair_r.at[0], sibling)

    def t_copy(peer):
        return copy(parts.at[row], parts.at[row], t_send.at[peer], t_recv.at[row], (peer // groups, peer % groups, depth))

    def to_peers(act):
        def one(peer):
            @pl.when(peer != row * groups + col)
            def _():
                act(t_copy(peer))
        loop(0, groups * groups, one)

    def send_traces():
        pair_copy().wait_recv()
        parts[row] = pair[0] + pair[1]
        to_peers(lambda c: c.start())

    def loop(begin, end_at, body):
        def one(index, carry):
            body(index)
            return carry
        lax.fori_loop(begin, end_at, one, 0)

    def tell(stage, target):
        pl.semaphore_signal(ready.at[stage], inc=1, device_id=target, device_id_type=MESH)

    def hear(stage):
        pl.semaphore_wait(ready.at[stage], 1)

    def plane_sent():
        for axis in range(2):
            for index in range(CHUNKS):
                near(axis, index).wait_send()
                near_place(axis, index, depth)[1].wait_send()
            for index in range(PIECES):
                @pl.when(goes_far(axis, index))
                def _(axis=axis, index=index):
                    far(axis, index).wait_send()
        for index in range(PIECES):
            far_place(index, depth)[1].wait_send()

    def outer_sent():
        plane_sent()
        loop(0, PIECES, lambda i: up(i).wait_send())

        lifts(lambda axis: lift(axis).wait_send())

    def given_sent():
        def sent(index):
            for axis in range(2):
                @pl.when(gives(axis, index))
                def _(axis=axis):
                    give(axis, index).wait_send()

                @pl.when(given(axis, index))
                def _(axis=axis):
                    give_place(axis, index, depth)[1].wait_send()

            @pl.when(mrow != 0)
            def _():
                own_share(index, depth).wait_send()

        loop(0, PIECES, sent)

    def inner_sent():
        plane_sent()

        def sent(index):
            for which in range(2):
                cross(which, index).wait_send()
            for which in range(3):
                @pl.when(goes_down(which, index))
                def _(which=which):
                    down(which, index).wait_send()

        loop(0, PIECES, sent)
        loop(0, PIECES - WHOLE, lambda i: down_part(i).wait_send())
        pl.when(mrow == 0)(lambda: hint_copy().wait_send())
        lifts(lambda axis: lift_place(axis, depth)[1].wait_send())

    def near_ready(axis, begin, end_at):
        for index in range(begin, end_at):
            near_place(axis, index, 1 - depth)[1].wait_recv()
        split(right.at[beside[axis]], beside[axis], 2 * begin, 2 * (end_at - begin))

    def near_part(axis, begin, end_at):
        near_ready(axis, begin, end_at)
        accumulate(beside[axis], 0, CHUNKS, pl.ds(2 * begin * BS, 2 * (end_at - begin) * BS))

    @pl.when(outer)
    def _():
        def rest_up():
            loop(PIECES - per_block, PIECES, lambda i: up(i).start())

        for index in range(CHUNKS):
            if index:
                ordered(index)
            if index < CHUNKS - 1:
                loop(per_block * index, per_block * (index + 1), lambda i: up(i).start())
            else:
                pl.when(mrow != 0)(rest_up)
            for axis in range(2):
                near(axis, index).start()
        tell(0, plane[0])
        take_blocks(range(CHUNKS, panel))
        total[...] = jnp.zeros_like(total)
        split(tile, row, 0, panel)
        for index in range(CHUNKS):
            for axis in range(2):
                take_near(axis, index)
            if index == 0:
                hear(0)
                tell(1, plane[1])
            if index == 1:
                @pl.when(mrow == 0)
                def _():
                    lifts(lambda axis: lift(axis).start())
                    rest_up()

                hear(1)
                tell(2, partner)

        @pl.when(mrow != 0)
        def _():
            lifts(lambda axis: lift(axis).start())

        for index in range(CHUNKS):
            for axis in range(2):
                near_place(axis, index, 1 - depth)[1].wait_recv()
        for axis in range(2):
            split(right.at[beside[axis]], beside[axis], 0, panel)
        for index in range(CHUNKS):
            take_far(index)
        for index in range(CHUNKS):
            far_shared(index)
        split(right.at[corner], corner, 0, panel)
        accumulate(end, 0, CHUNKS)

        def arrived(which, index):
            @pl.when(goes_down(which, index))
            def _():
                place = left.at[(mid, group1, group2)[which], some(index)]
                copy(place, place, down_s.at[which, index], down_r.at[which, index], sibling).wait_recv()

        for which in range(3):
            loop(0, PIECES, lambda i: arrived(which, i))
            if which == 1:
                accumulate(direct, 0, CHUNKS)
                accumulate(summed, 0, 1)
        accumulate(group2, 0, 1)
        loop(0, WHOLE, finish)

        @pl.when(mrow == 0)
        def _():
            pair[0] = block_traces()

        def last(index):
            at = some(index)
            place = partial_in.at[at]
            copy(place, place, part_s.at[index], part_r.at[index], sibling).wait_recv()
            value = partial_in[at]
            for slot in range(slots):
                total[slot, some(index + WHOLE)] += value[:, slot * BS:(slot + 1) * BS]
            finish(index + WHOLE)

        loop(0, PIECES - WHOLE - 1, last)

        @pl.when(mrow == 0)
        def _():
            copy(hint, hint_in, hint_s.at[0], hint_r.at[0], sibling).wait_recv()
            pair[0] = pair[0] + hint_in[...]
            pair_copy().start()
            hear(4)
            send_traces()

        pl.when(mrow != 0)(lambda: hear(4))
        outer_sent()
        last(PIECES - WHOLE - 1)

    @pl.when(jnp.logical_not(outer))
    def _():
        for index in range(CHUNKS):
            first_piece, last_piece = per_block * index, per_block * (index + 1)
            if index:
                ordered(index)

            def own_cross():
                loop(first_piece, last_piece, lambda i: cross(0, i).start())

            def own_down():
                loop(first_piece, last_piece, lambda i: down(0, i).start())

            if last_piece <= WHOLE:
                own_cross()
                own_down()
            else:
                pl.when(mrow != 3)(own_cross)
                pl.when(mrow >= 2)(own_down)
            for axis in range(2):
                if index:
                    pl.when(jnp.logical_not(gives_at_all[axis]))(lambda: near(axis, index).start())
                else:
                    near(axis, index).start()
        tell(0, plane[0])
        take_blocks(range(CHUNKS, panel))
        total[...] = jnp.zeros_like(total)
        split(tile, row, 0, panel)

        mrow_there = (mrow_x, mrow_y)

        def pass_up(index):
            up(index).wait_recv()
            cross(1, index).start()

        def first(index):
            @pl.when(jnp.logical_or(mrow != 0, index < PIECES - per_block))
            def _():
                pass_up(index)

            for axis in range(2):
                @pl.when(gives(axis, index))
                def _(axis=axis):
                    give(axis, index).start()

                for turn in range(1, CHUNKS):
                    moment = jnp.where(mrow_there[axis] == 0, (1, 5)[turn - 1], 3)

                    @pl.when(jnp.logical_and(gives_at_all[axis], index == moment))
                    def _(axis=axis, turn=turn):
                        near(axis, turn).start()

            @pl.when(mrow != 0)
            def _():
                own_share(index, depth).start()

            cross_in(False, index).wait_recv()

            @pl.when(goes_down(1, index))
            def _():
                down(1, index).start()

            @pl.when(index == 1)
            def _():
                for axis in range(2):
                    take_near(axis, 0, False)
                for axis in range(2):
                    pl.when(jnp.logical_not(gives_at_all[axis]))(functools.partial(pass_far, axis, 0))

            @pl.when(jnp.logical_and(mrow == 0, index == PIECES - 2))
            def _():
                for axis in range(2):
                    take_near(axis, 1)

            @pl.when(index >= 2)
            def _():
                for axis in range(2):
                    take_given(axis, index - 2)

        def whole_group2(index):
            cross_in(True, index).wait_recv()
            down(2, index).start()

        pl.when(mrow == 0)(lambda: loop(0, WHOLE, whole_group2))
        loop(0, PIECES, first)

        @pl.when(mrow == 3)
        def _():
            loop(WHOLE, PIECES, lambda i: cross(0, i).start())

        for axis in range(2):
            pl.when(gives_at_all[axis])(functools.partial(pass_far, axis, 0))
        hear(0)
        tell(1, plane[1])
        early = (mrow == 1, mrow >= 2)
        for axis in range(2):
            @pl.when(early[axis])
            def _(axis=axis):
                for turn in range(1, CHUNKS):
                    take_near(axis, turn)

        @pl.when(jnp.logical_or(mrow == 1, mrow == 2))
        def _():
            accumulate(row, 0, CHUNKS)

        @pl.when(mrow == 3)
        def _():
            near_part(1, 0, CHUNKS)

        for index in range(WHOLE):
            pl.when(mrow != 0)(functools.partial(whole_group2, index))
            for axis in range(2):
                take_given(axis, PIECES - 2 + index)

        def take_lift(axis):
            place, share = lift_place(axis, depth)
            copy(place, place, lift_s.at[axis], lift_r.at[axis], sibling).wait_recv()
            share.start()

        def shared(index):
            for axis in range(2):
                @pl.when(given(axis, index))
                def _(axis=axis):
                    give_place(axis, index, 1 - depth)[1].wait_recv()

            @pl.when(mrow != 0)
            def _():
                own_share(index, 1 - depth).wait_recv()

        loop(0, PIECES, shared)

        @pl.when(mrow != 0)
        def _():
            for index in range(CHUNKS):
                extra[own_slot, chunk(index, depth)] = left[end, index * BS:(index + 1) * BS]

        def split_extra(slot, turn):
            split(extra.at[slot], groups + slot, 2 * turn, 2)

        from_z = (
            (mrow == 0, 0, 1), (mrow == 0, 1, 1), (mrow == 3, 0, CHUNKS - 1),
            (jnp.logical_or(mrow == 1, mrow == 2), 1, CHUNKS - 1),
        )
        for slot in range(2):
            for turn in range(CHUNKS):
                late = [condition for condition, *which in from_z if which == [slot, turn]]
                if late:
                    pl.when(jnp.logical_not(late[0]))(functools.partial(split_extra, slot, turn))
                else:
                    split_extra(slot, turn)

        later_rows = slice(WHOLE * piece, None)

        def begin_part(begin, end_at, add=True):
            at = pl.ds(2 * begin * BS, 2 * (end_at - begin) * BS)
            result = times(left[summed, later_rows, at], groups, at)
            partial[...] = partial[...] + result if add else result

        @pl.when(jnp.logical_or(mrow == 1, mrow == 2))
        def _():
            begin_part(0, CHUNKS, False)

        @pl.when(mrow == 3)
        def _():
            begin_part(0, 2, False)

        @pl.when(mrow == 0)
        def _():
            begin_part(0, 1, False)
            begin_part(2, CHUNKS)

        given_sent()
        lifts(take_lift)
        lifts(lambda axis: lift_place(axis, 1 - depth)[1].wait_recv())
        for condition, slot, turn in from_z:
            pl.when(condition)(functools.partial(split_extra, slot, turn))
        pl.when(mrow == 0)(lambda: begin_part(1, 2))
        pl.when(mrow == 3)(lambda: begin_part(2, CHUNKS))
        hear(1)

        def send_part(index):
            cross_in(True, index).wait_recv()
            at = some(index - WHOLE)
            partial[at] += times(left[group2, some(index)], groups + 1, everything)

            @pl.when(jnp.logical_and(mrow == 0, index == PIECES - 1))
            def _():
                hint[...] = partial_traces()
                hint_copy().start()

            down_part(index - WHOLE).start()

        def corner_part(turn):
            take_far(turn)
            far_shared(turn)
            split(right.at[corner], corner, 2 * turn, 2)
            if turn < CHUNKS - 1:
                accumulate(corner, 0, CHUNKS, pl.ds(2 * turn * BS, 2 * BS))

        send_part(WHOLE)
        pl.when(mrow == 0)(lambda: pass_up(PIECES - 2))
        for axis in range(2):
            @pl.when(jnp.logical_and(mrow != 0, jnp.logical_not(early[axis])))
            def _(axis=axis):
                take_near(axis, 1)

        @pl.when(mrow == 0)
        def _():
            near_part(0, 0, 2)
            accumulate(row, 0, 1)

        @pl.when(mrow == 1)
        def _():
            near_part(0, 0, CHUNKS)

        @pl.when(mrow == 2)
        def _():
            near_part(1, 0, CHUNKS)

        @pl.when(mrow == 3)
        def _():
            near_part(0, 0, 2)

        hear(2)
        tell(3, opposite)
        send_part(WHOLE + 1)
        pl.when(mrow == 0)(lambda: pass_up(PIECES - 1))
        for axis in range(2):
            @pl.when(jnp.logical_not(early[axis]))
            def _(axis=axis):
                take_near(axis, 2)

        @pl.when(mrow == 0)
        def _():
            accumulate(row, 1, 2)

        @pl.when(jnp.logical_or(mrow == 0, mrow == 3))
        def _():
            near_part(0, 2, CHUNKS)

        @pl.when(mrow != 0)
        def _():
            corner_part(0)

        send_part(WHOLE + 2)
        hear(3)
        tell(4, partner)

        @pl.when(mrow < 2)
        def _():
            near_ready(1, 0, CHUNKS)

        @pl.when(mrow == 2)
        def _():
            near_ready(0, 0, CHUNKS)

        accumulate(group2, 0, 2)

        @pl.when(mrow != 0)
        def _():
            corner_part(1)

        send_part(WHOLE + 3)
        accumulate(group2, 2, 1)

        @pl.when(mrow == 0)
        def _():
            corner_part(0)
            corner_part(1)

        corner_part(2)
        at = pl.ds(2 * (CHUNKS - 1) * BS, 2 * BS)

        def last_block(index):
            accumulate(corner, index, 1, at)
            loop(per_block * index, per_block * (index + 1), finish)

        pl.when(mrow != 1)(lambda: loop(0, CHUNKS, last_block))

        @pl.when(mrow == 1)
        def _():
            accumulate(corner, 0, CHUNKS, at)
            pair[0] = block_traces()
            pair_copy().start()
            loop(0, PIECES - per_block, finish)
            send_traces()
            loop(PIECES - per_block, PIECES, finish)


    for source in range(groups):
        @pl.when(jnp.logical_or(row != source, col != source))
        def _(source=source):
            copy(parts.at[source], parts.at[source], t_send.at[source], t_recv.at[source], sibling).wait_recv()
    sum_all = parts[0]
    for source in range(1, groups):
        sum_all = sum_all + parts[source]
    trace_ref[...] = sum_all

    @pl.when(row == col)
    def _():
        pair_copy().wait_send()
        to_peers(lambda c: c.wait_send())

    pl.when(jnp.logical_not(outer))(inner_sent)

    def last_share(index):
        out_share(index, 1 - depth).wait_recv()
        out_share(index, depth).wait_send()

    loop(0, PIECES, last_share)


def full_rows(groups, blocks, columns, branch):
    panel, _, slots = blocks.shape[:3]
    size = panel * BS
    half = size // 2
    later = half - WHOLE * (half // PIECES)
    sems = pltpu.SemaphoreType.DMA
    vmem = pl.BlockSpec(memory_space=pltpu.VMEM)
    smem = pl.BlockSpec(memory_space=pltpu.SMEM)

    def both(*shape):
        return [sems(shape), sems(shape)]

    updated, traces = pl.pallas_call(
        square_kernel,
        out_shape=(
            pltpu.VMEM(blocks.shape, jnp.float32),
            pltpu.VMEM((8, BS), jnp.float32),
        ),
        in_specs=[smem, smem, pl.BlockSpec(memory_space=pl.ANY)],
        out_specs=(vmem, vmem),
        scratch_shapes=[
            pltpu.VMEM((panel // 2, slots, BS, BS), jnp.float32),
            pltpu.VMEM((panel // 2, slots, BS, BS), jnp.float32),
            pltpu.VMEM((size, size), jnp.float32),
            pltpu.VMEM((groups, half, size), jnp.float32),
            pltpu.VMEM((groups, size, size), jnp.float32),
            pltpu.VMEM((2, size, size), jnp.float32),
            pltpu.VMEM((groups + 2, size, size), jnp.bfloat16),
            pltpu.VMEM((groups + 2, size, size), jnp.bfloat16),
            pltpu.VMEM((slots, half, BS), jnp.float32),
            pltpu.VMEM((later, size), jnp.float32),
            pltpu.VMEM((later, size), jnp.float32),
            pltpu.VMEM((2, 8, BS), jnp.float32),
            pltpu.VMEM((8, BS), jnp.float32),
            pltpu.VMEM((8, BS), jnp.float32),
            pltpu.VMEM((groups, 8, BS), jnp.float32),
            sems((panel,)),
            *both(2, PIECES),
            *both(PIECES),
            *both(3, PIECES),
            *both(PIECES - WHOLE),
            *both(2, CHUNKS),
            sems((2, PIECES)),
            sems((PIECES,)),
            *both(2, PIECES),
            *both(2),
            *both(2, CHUNKS),
            *both(PIECES),
            *both(2, PIECES),
            *both(PIECES),
            *both(2),
            *both(PIECES),
            *both(1),
            *both(1),
            sems((groups * groups,)),
            sems((groups,)),
            pltpu.SemaphoreType.REGULAR((5,)),
        ],
        compiler_params=pltpu.CompilerParams(
            collective_id=0, has_side_effects=True, vmem_limit_bytes=60 * 2**20
        ),
    )(columns, branch, blocks)
    return updated, traces[0, :2]


def solution(mesh):
    placed = (P("row", "col", None, None, None), P("row", "col", None), P("row"))
    grid = mesh.shape["row"], mesh.shape["col"], mesh.shape["depth"]

    def per_device(blocks, columns, branch):
        panel, _, slots = blocks.shape[:3]
        if grid[0] == 4 and grid[1] == 4 and grid[2] == 2 and panel == slots == 2 * CHUNKS:
            return full_rows(grid[1], blocks, columns, branch)
        return on_device(blocks, columns, branch)

    return jax.shard_map(
        per_device,
        mesh=mesh,
        in_specs=placed,
        out_specs=(P("row", "col", None, None, None), P()),
        check_vma=False,
    )
```

```python
import functools

import jax
import jax.numpy as jnp
from jax import lax
from jax.experimental import pallas as pl
from jax.experimental.pallas import tpu as pltpu
from jax.sharding import PartitionSpec as P

BS = 128
SPG = 6


EXACT = lax.Precision.HIGHEST


def shifted(value, axis, steps):
    count = lax.axis_size(axis)
    pairs = [(source, (source + steps) % count) for source in range(count)]
    return lax.ppermute(value, axis, pairs)


def cannon_sum(a_blocks, a_cols, out_cols, moving, moving_cols, offset, panel, passer):
    grid_rows = lax.axis_size("row")
    my_row = lax.axis_index("row")
    out_count = a_blocks.shape[0]
    slot_total = a_blocks.shape[1] * a_blocks.shape[2]
    a_flat = a_blocks.reshape(out_count, slot_total, BS, BS)
    a_cflat = a_cols.reshape(out_count, slot_total)
    tile_rows = moving.shape[0]
    start_sum = jnp.zeros((out_count, SPG, BS, BS), jnp.float32)

    def contribute(running, pieces, piece_cols, step_index):
        source = (my_row - step_index) % grid_rows
        wanted = source * panel + offset + jnp.arange(tile_rows, dtype=jnp.int32)
        hits = (a_cflat[:, :, None] == wanted[None, None, :]).astype(jnp.float32)
        stacked = jnp.einsum("nst,nsxy->tnxy", hits, a_flat, precision=EXACT)
        matches = (piece_cols[:, None, None, :] == out_cols[None, :, :, None]).astype(jnp.float32)

        def one_tile_row(total, items):
            left_side, right_side, pairing = items
            products = jnp.einsum("nxy,byz->nbxz", left_side, right_side, precision=EXACT)
            return (total + jnp.einsum("njb,nbxz->njxz", pairing, products, precision=EXACT), 0)

        running, unused = lax.scan(one_tile_row, running, (stacked, pieces, matches))
        return running

    def turn(step_index, carry):
        running, pieces, piece_cols = carry
        running = contribute(running, pieces, piece_cols, step_index)
        pieces, piece_cols = passer(pieces, piece_cols)
        return (running, pieces, piece_cols)

    running, pieces, piece_cols = lax.fori_loop(
        0, grid_rows - 1, turn, (start_sum, moving, moving_cols)
    )
    return contribute(running, pieces, piece_cols, grid_rows - 1)


def pass_whole(pieces, piece_cols):
    return shifted((pieces, piece_cols), "row", 1)


def on_device(blocks, columns, branch):
    panel = blocks.shape[0]
    layer_count = lax.axis_size("depth")
    layer = lax.axis_index("depth")
    my_row = lax.axis_index("row")
    rows_half = panel // layer_count
    first_row = layer * rows_half
    own_blocks = blocks[:, 0]
    own_cols = columns[:, 0]
    half_blocks = lax.dynamic_slice_in_dim(blocks, first_row, rows_half, 0)
    half_cols = lax.dynamic_slice_in_dim(columns, first_row, rows_half, 0)
    a_blocks, a_cols = (
        lax.all_gather(half_blocks, "col", axis=1, tiled=True),
        lax.all_gather(half_cols, "col", axis=1, tiled=True),
    )
    partial_sum = cannon_sum(
        a_blocks, a_cols, half_cols[:, 0], own_blocks, own_cols, 0, panel, pass_whole
    )
    product = lax.all_gather(partial_sum, "depth", axis=0, tiled=True)
    chooser = (branch == 1)[:, None, None, None]
    updated = jnp.where(chooser, product, 2.0 * own_blocks - product)
    row_ids = my_row * panel + jnp.arange(panel, dtype=jnp.int32)
    on_diag = (own_cols == row_ids[:, None]).astype(jnp.float32)
    old_term = jnp.sum(on_diag * jnp.trace(own_blocks, axis1=2, axis2=3))
    new_term = jnp.sum(on_diag * jnp.trace(updated, axis1=2, axis2=3))
    traces = lax.psum(jnp.stack([old_term, new_term]), ("row", "col"))
    return (updated[:, None], traces)


MESH = pl.DeviceIdType.MESH
PIECES = 6
WHOLE = 2
CHUNKS = 3


def halves(value):
    high = value.astype(jnp.bfloat16)
    return high, (value - high.astype(jnp.float32)).astype(jnp.bfloat16)


def square_kernel(
    cols_ref, branch_ref, blocks_hbm, out_ref, trace_ref,
    mine, others, tile, left, right, extra, high_ref, low_ref, total, partial, partial_in, pair, hint, hint_in, parts,
    in_sem, cross_s, cross_r, up_s, up_r, down_s, down_r, part_s, part_r,
    near_s, near_r, far_s, far_r, give_s, give_r, lift_s, lift_r,
    near_ss, near_sr, far_ss, far_sr, give_ss, give_sr, own_ss, own_sr, lift_ss, lift_sr,
    out_s, out_r, hint_s, hint_r, pair_s, pair_r, t_send, t_recv, ready,
):
    row, col, depth = lax.axis_index("row"), lax.axis_index("col"), lax.axis_index("depth")
    panel, slots = 2 * mine.shape[0], mine.shape[1]
    groups = parts.shape[0]
    size = tile.shape[0]
    half = size // 2
    piece = half // PIECES
    per_block = BS // piece
    side = col // 2

    def mirrored(value):
        return value + side * (3 - 2 * value)

    mrow, mcol = mirrored(row), mirrored(col)
    outer = mcol == 0
    end, mid, mid2, end2 = mirrored(0), mirrored(1), mirrored(2), mirrored(3)
    group1 = jnp.where(mrow == 0, end2, mid2)
    group2 = jnp.where(mrow == 0, mid2, end2)
    direct = jnp.where(mrow < 2, group1, mid)
    summed = jnp.where(mrow < 2, mid, group1)
    x_row, y_row, corner = row + 1 - 2 * (row % 2), (row + 2) % 4, 3 - row
    mrow_x, mrow_y = mrow + 1 - 2 * (mrow % 2), (mrow + 2) % 4
    beside = (x_row, y_row)
    sibling = (row, col, 1 - depth)
    plane = ((x_row, col, depth), (y_row, col, depth))
    partner = (row, col + 1 - 2 * (col % 2), depth)
    opposite = (row, 3 - col, depth)

    barrier = pltpu.get_barrier_semaphore()
    for peer in (sibling,) + plane + (partner,):
        pl.semaphore_signal(barrier, inc=1, device_id=peer, device_id_type=MESH)

    @pl.when(jnp.logical_not(outer))
    def _():
        pl.semaphore_signal(barrier, inc=1, device_id=opposite, device_id_type=MESH)

    def incoming(turn):
        block = 2 * (turn % CHUNKS) + (depth + turn // CHUNKS) % 2
        place = mine if turn < CHUNKS else others
        return block, pltpu.make_async_copy(blocks_hbm.at[block, 0], place.at[turn % CHUNKS], in_sem.at[turn])

    def ordered(turn):
        block = incoming(turn)[0]
        place = mine if turn < CHUNKS else others
        at = pl.ds(pl.multiple_of(block * BS, BS), BS)
        for target_slot in range(slots):
            source = 0
            for slot in range(1, slots):
                source = jnp.where(lax.rem(cols_ref[block, 0, slot], slots) == target_slot, slot, source)
            value = place[turn % CHUNKS, source]
            tile[at, target_slot * BS:(target_slot + 1) * BS] = value
            if turn < CHUNKS:
                left[col, turn * BS:(turn + 1) * BS, target_slot * BS:(target_slot + 1) * BS] = value

    def take_blocks(turns):
        for turn in turns:
            incoming(turn)[1].wait()
        for turn in turns:
            ordered(turn)

    for turn in range(CHUNKS):
        incoming(turn)[1].start()
    for turn in range(CHUNKS):
        incoming(turn)[1].wait()
    for turn in range(CHUNKS, panel):
        incoming(turn)[1].start()
    ordered(0)
    pl.semaphore_wait(barrier, jnp.where(outer, 4, 5))

    def copy(src, dst, send, recv, target):
        return pltpu.make_async_remote_copy(
            src_ref=src, dst_ref=dst, send_sem=send, recv_sem=recv, device_id=target, device_id_type=MESH
        )

    def some(index, count=1):
        return pl.ds(pl.multiple_of(index * piece, piece), count * piece)

    def spot(index, core):
        start = (2 * (index // per_block) + core) * BS + (index % per_block) * piece
        return pl.ds(pl.multiple_of(start, piece), piece)

    def chunk(index, core):
        return pl.ds(pl.multiple_of((2 * index + core) * BS, BS), BS)

    def cross(which, index):
        place = left.at[col if which == 0 else end, some(index)]
        return copy(place, place, cross_s.at[which, index], cross_r.at[which, index], opposite)

    def cross_in(second, index):
        which = jnp.where((mrow == 0) != second, 1, 0)
        place = left.at[group2 if second else group1, some(index)]
        return copy(place, place, cross_s.at[which, index], cross_r.at[which, index], sibling)

    def up(index):
        place = left.at[end, some(index)]
        return copy(place, place, up_s.at[index], up_r.at[index], partner)

    def down(which, index):
        place = left.at[(mid, group1, group2)[which], some(index)]
        return copy(place, place, down_s.at[which, index], down_r.at[which, index], partner)

    def goes_down(which, index):
        whole = index < WHOLE
        if which == 2:
            return whole
        return jnp.logical_or(whole, mrow >= 2 if which == 0 else mrow < 2)

    def down_part(index):
        at = some(index)
        return copy(partial.at[at], partial_in.at[at], part_s.at[index], part_r.at[index], partner)

    def near(axis, index):
        at = chunk(index, depth)
        return copy(tile.at[at], right.at[row, at], near_s.at[axis, index], near_r.at[axis, index], plane[axis])

    def near_place(axis, index, core):
        place = right.at[beside[axis], chunk(index, core)]
        return place, copy(place, place, near_ss.at[axis, index], near_sr.at[axis, index], sibling)

    def far(axis, index):
        place = right.at[beside[1 - axis], spot(index, depth)]
        return copy(place, place, far_s.at[axis, index], far_r.at[index], plane[axis])

    def goes_far(axis, index):
        who = (mrow_x, mrow_y)[axis]
        turn, part = index // per_block, index % per_block
        by_x = turn == 0 or (turn == CHUNKS - 1 and part == 0)
        mixed = jnp.logical_or(outer, who == 0)
        if by_x == (axis == 0):
            return jnp.logical_or(mixed, who == 1 if axis == 0 else who >= 2)
        return jnp.logical_and(jnp.logical_not(mixed), who == 1 if axis == 0 else who >= 2)

    def far_place(index, core):
        place = right.at[corner, spot(index, core)]
        return place, copy(place, place, far_ss.at[index], far_sr.at[index], sibling)

    def parts_of(turn):
        return range(per_block * turn, per_block * (turn + 1))

    def take_near(axis, index, forward=True):
        place, share = near_place(axis, index, depth)
        copy(place, place, near_s.at[axis, index], near_r.at[axis, index], sibling).wait_recv()
        share.start()
        if forward:
            pass_far(1 - axis, index)

    def pass_far(axis, turn):
        for index in parts_of(turn):
            @pl.when(goes_far(axis, index))
            def _(index=index):
                far(axis, index).start()

    def take_far(turn):
        for index in parts_of(turn):
            place, share = far_place(index, depth)
            copy(place, place, far_s.at[0, index], far_r.at[index], sibling).wait_recv()
            share.start()

    def far_shared(turn):
        for index in parts_of(turn):
            far_place(index, 1 - depth)[1].wait_recv()

    x_slot = jnp.where(mrow == 2, 1, 0)
    x_slot_there = jnp.where(mrow_x == 2, 1, 0)
    own_slot = jnp.where(mrow == 3, 1, 0)

    def give(axis, index):
        slot = x_slot_there if axis == 0 else 1
        return copy(
            left.at[end, some(index)], extra.at[slot, spot(index, depth)],
            give_s.at[axis, index], give_r.at[axis, index], plane[axis],
        )

    def lifted(who):
        return jnp.where(who == 0, 1, CHUNKS - 1)

    gives_at_all = (mrow != 0, mrow >= 2)
    given_at_all = (mrow != 1, mrow < 2)

    def gives(axis, index):
        return jnp.logical_and(gives_at_all[axis], index // per_block != lifted((mrow_x, mrow_y)[axis]))

    def given(axis, index):
        return jnp.logical_and(given_at_all[axis], index // per_block != lifted(mrow))

    def give_place(axis, index, core):
        place = extra.at[x_slot if axis == 0 else 1, spot(index, core)]
        return place, copy(place, place, give_ss.at[axis, index], give_sr.at[axis, index], sibling)

    def take_given(axis, index):
        @pl.when(given(axis, index))
        def _():
            place, share = give_place(axis, index, depth)
            copy(place, place, give_s.at[axis, index], give_r.at[axis, index], sibling).wait_recv()
            share.start()

    def own_share(index, core):
        return copy(
            left.at[end, some(index)], extra.at[own_slot, spot(index, core)],
            own_ss.at[index], own_sr.at[index], sibling,
        )

    def lift(axis):
        at = chunk(lifted(mrow), depth)
        place = extra.at[x_slot if axis == 0 else 1, at]
        return copy(right.at[beside[axis], at], place, lift_s.at[axis], lift_r.at[axis], partner)

    def lift_place(axis, core):
        place = extra.at[x_slot if axis == 0 else 1, chunk(lifted(mrow), core)]
        return place, copy(place, place, lift_ss.at[axis], lift_sr.at[axis], sibling)

    def lifts(act):
        for axis in range(2):
            @pl.when(given_at_all[axis])
            def _(axis=axis):
                act(axis)

    def split(source, slot, begin, count):
        def one(part, carry):
            at = pl.ds(pl.multiple_of((begin + part) * BS, BS), BS)
            high_ref[slot, at], low_ref[slot, at] = halves(source[at])
            return carry
        lax.fori_loop(0, count, one, 0)

    dot = functools.partial(jnp.dot, preferred_element_type=jnp.float32)

    def times(value, slot, at):
        high, low = halves(value)
        return (dot(high, low_ref[slot, at]) + dot(low, high_ref[slot, at])) + dot(high, high_ref[slot, at])

    everything = pl.ds(0, size)

    def accumulate(group, begin, count, at=everything):
        if count == CHUNKS:
            result = times(left[group, :, at], group, at)
            for slot in range(slots):
                total[slot] += result[:, slot * BS:(slot + 1) * BS]
            return

        def one(part, carry):
            rows = pl.ds(pl.multiple_of((begin + part) * BS, BS), BS)
            result = times(left[group, rows, at], group, at)
            for slot in range(slots):
                total[slot, rows] += result[:, slot * BS:(slot + 1) * BS]
            return carry
        lax.fori_loop(0, count, one, 0)

    def block_of(index):
        return 2 * (index // per_block) + depth

    def out_share(index, core):
        inner = pl.ds((index % per_block) * piece, piece)
        place = out_ref.at[2 * (index // per_block) + core, 0, :, inner]
        return copy(place, place, out_s.at[index], out_r.at[index], sibling)

    def finish(index):
        block = block_of(index)
        inner = pl.ds(pl.multiple_of((index % per_block) * piece, piece), piece)
        taken = branch_ref[block] == 1
        for slot in range(slots):
            square = total[lax.rem(cols_ref[block, 0, slot], slots), some(index)]
            out_ref[block, 0, slot, inner] = jnp.where(taken, square, 2.0 * mine[index // per_block, slot, inner] - square)
        out_share(index, depth).start()

    eye = lax.broadcasted_iota(jnp.int32, (BS, BS), 0) == lax.broadcasted_iota(jnp.int32, (BS, BS), 1)
    lane = lax.broadcasted_iota(jnp.int32, parts.shape[1:], 1)

    def old_and_new(old_sum, new_sum):
        old_all = jnp.sum(jnp.where(eye, old_sum, 0.0))
        new_all = jnp.sum(jnp.where(eye, new_sum, 0.0))
        return jnp.where(lane == 0, old_all, jnp.where(lane == 1, new_all, 0.0))

    def block_traces():
        old_sum = jnp.zeros((BS, BS), jnp.float32)
        new_sum = jnp.zeros((BS, BS), jnp.float32)
        for index in range(CHUNKS):
            block = 2 * index + depth
            at = pl.ds(pl.multiple_of(block * BS, BS), BS)
            old = tile[at, at]
            square = total[block, index * BS:(index + 1) * BS]
            new_sum += jnp.where(branch_ref[block] == 1, square, 2.0 * old - square)
            old_sum += old
        return old_and_new(old_sum, new_sum)

    def partial_traces():
        new_sum = jnp.zeros((BS, BS), jnp.float32)
        for index in range(WHOLE // per_block, CHUNKS):
            block = 2 * index + depth
            start = index * BS - WHOLE * piece
            square = partial[start:start + BS, pl.ds(pl.multiple_of(block * BS, BS), BS)]
            new_sum += jnp.where(branch_ref[block] == 1, square, -square)
        return old_and_new(jnp.zeros((BS, BS), jnp.float32), new_sum)

    def hint_copy():
        return copy(hint, hint_in, hint_s.at[0], hint_r.at[0], partner)

    def pair_copy():
        return copy(pair.at[0], pair.at[1], pair_s.at[0], pair_r.at[0], sibling)

    def t_copy(peer):
        return copy(parts.at[row], parts.at[row], t_send.at[peer], t_recv.at[row], (peer // groups, peer % groups, depth))

    def to_peers(act):
        def one(peer):
            @pl.when(peer != row * groups + col)
            def _():
                act(t_copy(peer))
        loop(0, groups * groups, one)

    def send_traces():
        pair_copy().wait_recv()
        parts[row] = pair[0] + pair[1]
        to_peers(lambda c: c.start())

    def loop(begin, end_at, body):
        def one(index, carry):
            body(index)
            return carry
        lax.fori_loop(begin, end_at, one, 0)

    def tell(stage, target):
        pl.semaphore_signal(ready.at[stage], inc=1, device_id=target, device_id_type=MESH)

    def hear(stage):
        pl.semaphore_wait(ready.at[stage], 1)

    def plane_sent():
        for axis in range(2):
            for index in range(CHUNKS):
                near(axis, index).wait_send()
                near_place(axis, index, depth)[1].wait_send()
            for index in range(PIECES):
                @pl.when(goes_far(axis, index))
                def _(axis=axis, index=index):
                    far(axis, index).wait_send()
        for index in range(PIECES):
            far_place(index, depth)[1].wait_send()

    def outer_sent():
        plane_sent()
        loop(0, PIECES, lambda i: up(i).wait_send())

        lifts(lambda axis: lift(axis).wait_send())

    def given_sent():
        def sent(index):
            for axis in range(2):
                @pl.when(gives(axis, index))
                def _(axis=axis):
                    give(axis, index).wait_send()

                @pl.when(given(axis, index))
                def _(axis=axis):
                    give_place(axis, index, depth)[1].wait_send()

            @pl.when(mrow != 0)
            def _():
                own_share(index, depth).wait_send()

        loop(0, PIECES, sent)

    def inner_sent():
        plane_sent()

        def sent(index):
            for which in range(2):
                cross(which, index).wait_send()
            for which in range(3):
                @pl.when(goes_down(which, index))
                def _(which=which):
                    down(which, index).wait_send()

        loop(0, PIECES, sent)
        loop(0, PIECES - WHOLE, lambda i: down_part(i).wait_send())
        lifts(lambda axis: lift_place(axis, depth)[1].wait_send())

    def near_ready(axis, begin, end_at):
        for index in range(begin, end_at):
            near_place(axis, index, 1 - depth)[1].wait_recv()
        split(right.at[beside[axis]], beside[axis], 2 * begin, 2 * (end_at - begin))

    def near_part(axis, begin, end_at):
        near_ready(axis, begin, end_at)
        accumulate(beside[axis], 0, CHUNKS, pl.ds(2 * begin * BS, 2 * (end_at - begin) * BS))

    @pl.when(outer)
    def _():
        def rest_up():
            loop(PIECES - per_block, PIECES, lambda i: up(i).start())

        for index in range(CHUNKS):
            if index:
                ordered(index)
            if index < CHUNKS - 1:
                loop(per_block * index, per_block * (index + 1), lambda i: up(i).start())
            else:
                pl.when(mrow != 0)(rest_up)
            for axis in range(2):
                near(axis, index).start()
        tell(0, plane[0])
        take_blocks(range(CHUNKS, panel))
        total[...] = jnp.zeros_like(total)
        split(tile, row, 0, panel)
        for index in range(CHUNKS):
            for axis in range(2):
                take_near(axis, index)
            if index == 0:
                hear(0)
                tell(1, plane[1])
            if index == 1:
                @pl.when(mrow == 0)
                def _():
                    lifts(lambda axis: lift(axis).start())
                    rest_up()

                hear(1)
                tell(2, partner)

        @pl.when(mrow != 0)
        def _():
            lifts(lambda axis: lift(axis).start())

        for index in range(CHUNKS):
            for axis in range(2):
                near_place(axis, index, 1 - depth)[1].wait_recv()
        for axis in range(2):
            split(right.at[beside[axis]], beside[axis], 0, panel)
        for index in range(CHUNKS):
            take_far(index)
        for index in range(CHUNKS):
            far_shared(index)
        split(right.at[corner], corner, 0, panel)
        accumulate(end, 0, CHUNKS)

        def arrived(which, index):
            @pl.when(goes_down(which, index))
            def _():
                place = left.at[(mid, group1, group2)[which], some(index)]
                copy(place, place, down_s.at[which, index], down_r.at[which, index], sibling).wait_recv()

        for which in range(3):
            loop(0, PIECES, lambda i: arrived(which, i))
            if which == 1:
                accumulate(direct, 0, CHUNKS)
                accumulate(summed, 0, 1)
        accumulate(group2, 0, 1)
        loop(0, WHOLE, finish)

        @pl.when(mrow == 0)
        def _():
            hint[...] = block_traces()
            hint_copy().start()

        def last(index):
            at = some(index)
            place = partial_in.at[at]
            copy(place, place, part_s.at[index], part_r.at[index], sibling).wait_recv()
            value = partial_in[at]
            for slot in range(slots):
                total[slot, some(index + WHOLE)] += value[:, slot * BS:(slot + 1) * BS]
            finish(index + WHOLE)

        outer_sent()
        loop(0, PIECES - WHOLE, last)
        pl.when(mrow == 0)(lambda: hint_copy().wait_send())

    @pl.when(jnp.logical_not(outer))
    def _():
        for index in range(CHUNKS):
            first_piece, last_piece = per_block * index, per_block * (index + 1)
            if index:
                ordered(index)

            def own_cross():
                loop(first_piece, last_piece, lambda i: cross(0, i).start())

            def own_down():
                loop(first_piece, last_piece, lambda i: down(0, i).start())

            if last_piece <= WHOLE:
                own_cross()
                own_down()
            else:
                pl.when(mrow != 3)(own_cross)
                pl.when(mrow >= 2)(own_down)
            for axis in range(2):
                if index:
                    pl.when(jnp.logical_not(gives_at_all[axis]))(lambda: near(axis, index).start())
                else:
                    near(axis, index).start()
        tell(0, plane[0])
        take_blocks(range(CHUNKS, panel))
        total[...] = jnp.zeros_like(total)
        split(tile, row, 0, panel)

        mrow_there = (mrow_x, mrow_y)

        def pass_up(index):
            up(index).wait_recv()
            cross(1, index).start()

        def first(index):
            @pl.when(jnp.logical_or(mrow != 0, index < PIECES - per_block))
            def _():
                pass_up(index)

            for axis in range(2):
                @pl.when(gives(axis, index))
                def _(axis=axis):
                    give(axis, index).start()

                for turn in range(1, CHUNKS):
                    moment = jnp.where(mrow_there[axis] == 0, (1, 5)[turn - 1], 3)

                    @pl.when(jnp.logical_and(gives_at_all[axis], index == moment))
                    def _(axis=axis, turn=turn):
                        near(axis, turn).start()

            @pl.when(mrow != 0)
            def _():
                own_share(index, depth).start()

            cross_in(False, index).wait_recv()

            @pl.when(goes_down(1, index))
            def _():
                down(1, index).start()

            @pl.when(index == 1)
            def _():
                for axis in range(2):
                    take_near(axis, 0, False)
                for axis in range(2):
                    pl.when(jnp.logical_not(gives_at_all[axis]))(functools.partial(pass_far, axis, 0))

            @pl.when(jnp.logical_and(mrow == 0, index == PIECES - 2))
            def _():
                for axis in range(2):
                    take_near(axis, 1)

            @pl.when(index >= 2)
            def _():
                for axis in range(2):
                    take_given(axis, index - 2)

        def whole_group2(index):
            cross_in(True, index).wait_recv()
            down(2, index).start()

        pl.when(mrow == 0)(lambda: loop(0, WHOLE, whole_group2))
        loop(0, PIECES, first)

        @pl.when(mrow == 3)
        def _():
            loop(WHOLE, PIECES, lambda i: cross(0, i).start())

        for axis in range(2):
            pl.when(gives_at_all[axis])(functools.partial(pass_far, axis, 0))
        hear(0)
        tell(1, plane[1])
        early = (mrow == 1, mrow >= 2)
        for axis in range(2):
            @pl.when(early[axis])
            def _(axis=axis):
                for turn in range(1, CHUNKS):
                    take_near(axis, turn)

        @pl.when(jnp.logical_or(mrow == 1, mrow == 2))
        def _():
            accumulate(row, 0, CHUNKS)

        @pl.when(mrow == 3)
        def _():
            near_part(1, 0, CHUNKS)

        for index in range(WHOLE):
            pl.when(mrow != 0)(functools.partial(whole_group2, index))
            for axis in range(2):
                take_given(axis, PIECES - 2 + index)

        def take_lift(axis):
            place, share = lift_place(axis, depth)
            copy(place, place, lift_s.at[axis], lift_r.at[axis], sibling).wait_recv()
            share.start()

        def shared(index):
            for axis in range(2):
                @pl.when(given(axis, index))
                def _(axis=axis):
                    give_place(axis, index, 1 - depth)[1].wait_recv()

            @pl.when(mrow != 0)
            def _():
                own_share(index, 1 - depth).wait_recv()

        loop(0, PIECES, shared)

        @pl.when(mrow != 0)
        def _():
            for index in range(CHUNKS):
                extra[own_slot, chunk(index, depth)] = left[end, index * BS:(index + 1) * BS]

        def split_extra(slot, turn):
            split(extra.at[slot], groups + slot, 2 * turn, 2)

        from_z = (
            (mrow == 0, 0, 1), (mrow == 0, 1, 1), (mrow == 3, 0, CHUNKS - 1),
            (jnp.logical_or(mrow == 1, mrow == 2), 1, CHUNKS - 1),
        )
        for slot in range(2):
            for turn in range(CHUNKS):
                late = [condition for condition, *which in from_z if which == [slot, turn]]
                if late:
                    pl.when(jnp.logical_not(late[0]))(functools.partial(split_extra, slot, turn))
                else:
                    split_extra(slot, turn)

        later_rows = slice(WHOLE * piece, None)

        def begin_part(begin, end_at, add=True):
            at = pl.ds(2 * begin * BS, 2 * (end_at - begin) * BS)
            result = times(left[summed, later_rows, at], groups, at)
            partial[...] = partial[...] + result if add else result

        @pl.when(jnp.logical_or(mrow == 1, mrow == 2))
        def _():
            begin_part(0, CHUNKS, False)

        @pl.when(mrow == 3)
        def _():
            begin_part(0, 2, False)

        @pl.when(mrow == 0)
        def _():
            begin_part(0, 1, False)
            begin_part(2, CHUNKS)

        given_sent()
        lifts(take_lift)
        lifts(lambda axis: lift_place(axis, 1 - depth)[1].wait_recv())
        for condition, slot, turn in from_z:
            pl.when(condition)(functools.partial(split_extra, slot, turn))
        pl.when(mrow == 0)(lambda: begin_part(1, 2))
        pl.when(mrow == 3)(lambda: begin_part(2, CHUNKS))
        hear(1)

        def send_part(index):
            cross_in(True, index).wait_recv()
            at = some(index - WHOLE)
            partial[at] += times(left[group2, some(index)], groups + 1, everything)
            down_part(index - WHOLE).start()

        def corner_part(turn):
            take_far(turn)
            far_shared(turn)
            split(right.at[corner], corner, 2 * turn, 2)
            if turn < CHUNKS - 1:
                accumulate(corner, 0, CHUNKS, pl.ds(2 * turn * BS, 2 * BS))

        send_part(WHOLE)
        pl.when(mrow == 0)(lambda: pass_up(PIECES - 2))
        for axis in range(2):
            @pl.when(jnp.logical_and(mrow != 0, jnp.logical_not(early[axis])))
            def _(axis=axis):
                take_near(axis, 1)

        @pl.when(mrow == 0)
        def _():
            near_part(0, 0, 2)
            accumulate(row, 0, 1)

        @pl.when(mrow == 1)
        def _():
            near_part(0, 0, CHUNKS)

        @pl.when(mrow == 2)
        def _():
            near_part(1, 0, CHUNKS)

        @pl.when(mrow == 3)
        def _():
            near_part(0, 0, 2)

        hear(2)
        tell(3, opposite)
        send_part(WHOLE + 1)
        pl.when(mrow == 0)(lambda: pass_up(PIECES - 1))
        for axis in range(2):
            @pl.when(jnp.logical_not(early[axis]))
            def _(axis=axis):
                take_near(axis, 2)

        @pl.when(mrow == 0)
        def _():
            accumulate(row, 1, 2)

        @pl.when(jnp.logical_or(mrow == 0, mrow == 3))
        def _():
            near_part(0, 2, CHUNKS)

        @pl.when(mrow != 0)
        def _():
            corner_part(0)

        send_part(WHOLE + 2)
        hear(3)

        @pl.when(mrow < 2)
        def _():
            near_ready(1, 0, CHUNKS)

        @pl.when(mrow == 2)
        def _():
            near_ready(0, 0, CHUNKS)

        accumulate(group2, 0, 2)

        @pl.when(mrow != 0)
        def _():
            corner_part(1)

        send_part(WHOLE + 3)

        @pl.when(mrow == 0)
        def _():
            copy(hint, hint_in, hint_s.at[0], hint_r.at[0], sibling).wait_recv()
            pair[0] = partial_traces() + hint_in[...]
            pair_copy().start()

        accumulate(group2, 2, 1)

        @pl.when(mrow == 0)
        def _():
            corner_part(0)
            send_traces()
            corner_part(1)

        corner_part(2)
        at = pl.ds(2 * (CHUNKS - 1) * BS, 2 * BS)

        def last_block(index):
            accumulate(corner, index, 1, at)
            loop(per_block * index, per_block * (index + 1), finish)

        pl.when(mrow != 1)(lambda: loop(0, CHUNKS, last_block))

        @pl.when(mrow == 1)
        def _():
            accumulate(corner, 0, CHUNKS, at)
            pair[0] = block_traces()
            pair_copy().start()
            loop(0, PIECES - per_block, finish)
            send_traces()
            loop(PIECES - per_block, PIECES, finish)


    for source in range(groups):
        @pl.when(jnp.logical_or(row != source, col != min(max(source, 1), groups - 2)))
        def _(source=source):
            copy(parts.at[source], parts.at[source], t_send.at[source], t_recv.at[source], sibling).wait_recv()
    sum_all = parts[0]
    for source in range(1, groups):
        sum_all = sum_all + parts[source]
    trace_ref[...] = sum_all

    @pl.when(jnp.logical_and(jnp.logical_not(outer), mrow < 2))
    def _():
        pair_copy().wait_send()
        to_peers(lambda c: c.wait_send())

    pl.when(jnp.logical_not(outer))(inner_sent)

    def last_share(index):
        out_share(index, 1 - depth).wait_recv()
        out_share(index, depth).wait_send()

    loop(0, PIECES, last_share)


def full_rows(groups, blocks, columns, branch):
    panel, _, slots = blocks.shape[:3]
    size = panel * BS
    half = size // 2
    later = half - WHOLE * (half // PIECES)
    sems = pltpu.SemaphoreType.DMA
    vmem = pl.BlockSpec(memory_space=pltpu.VMEM)
    smem = pl.BlockSpec(memory_space=pltpu.SMEM)

    def both(*shape):
        return [sems(shape), sems(shape)]

    updated, traces = pl.pallas_call(
        square_kernel,
        out_shape=(
            pltpu.VMEM(blocks.shape, jnp.float32),
            pltpu.VMEM((8, BS), jnp.float32),
        ),
        in_specs=[smem, smem, pl.BlockSpec(memory_space=pl.ANY)],
        out_specs=(vmem, vmem),
        scratch_shapes=[
            pltpu.VMEM((panel // 2, slots, BS, BS), jnp.float32),
            pltpu.VMEM((panel // 2, slots, BS, BS), jnp.float32),
            pltpu.VMEM((size, size), jnp.float32),
            pltpu.VMEM((groups, half, size), jnp.float32),
            pltpu.VMEM((groups, size, size), jnp.float32),
            pltpu.VMEM((2, size, size), jnp.float32),
            pltpu.VMEM((groups + 2, size, size), jnp.bfloat16),
            pltpu.VMEM((groups + 2, size, size), jnp.bfloat16),
            pltpu.VMEM((slots, half, BS), jnp.float32),
            pltpu.VMEM((later, size), jnp.float32),
            pltpu.VMEM((later, size), jnp.float32),
            pltpu.VMEM((2, 8, BS), jnp.float32),
            pltpu.VMEM((8, BS), jnp.float32),
            pltpu.VMEM((8, BS), jnp.float32),
            pltpu.VMEM((groups, 8, BS), jnp.float32),
            sems((panel,)),
            *both(2, PIECES),
            *both(PIECES),
            *both(3, PIECES),
            *both(PIECES - WHOLE),
            *both(2, CHUNKS),
            sems((2, PIECES)),
            sems((PIECES,)),
            *both(2, PIECES),
            *both(2),
            *both(2, CHUNKS),
            *both(PIECES),
            *both(2, PIECES),
            *both(PIECES),
            *both(2),
            *both(PIECES),
            *both(1),
            *both(1),
            sems((groups * groups,)),
            sems((groups,)),
            pltpu.SemaphoreType.REGULAR((4,)),
        ],
        compiler_params=pltpu.CompilerParams(
            collective_id=0, has_side_effects=True, vmem_limit_bytes=60 * 2**20
        ),
    )(columns, branch, blocks)
    return updated, traces[0, :2]


def solution(mesh):
    placed = (P("row", "col", None, None, None), P("row", "col", None), P("row"))
    grid = mesh.shape["row"], mesh.shape["col"], mesh.shape["depth"]

    def per_device(blocks, columns, branch):
        panel, _, slots = blocks.shape[:3]
        if grid[0] == 4 and grid[1] == 4 and grid[2] == 2 and panel == slots == 2 * CHUNKS:
            return full_rows(grid[1], blocks, columns, branch)
        return on_device(blocks, columns, branch)

    return jax.shard_map(
        per_device,
        mesh=mesh,
        in_specs=placed,
        out_specs=(P("row", "col", None, None, None), P()),
        check_vma=False,
    )
```

```python
import functools

import jax
import jax.numpy as jnp
from jax import lax
from jax.experimental import pallas as pl
from jax.experimental.pallas import tpu as pltpu
from jax.sharding import PartitionSpec as P

BS = 128
SPG = 6


EXACT = lax.Precision.HIGHEST


def shifted(value, axis, steps):
    count = lax.axis_size(axis)
    pairs = [(source, (source + steps) % count) for source in range(count)]
    return lax.ppermute(value, axis, pairs)


def cannon_sum(a_blocks, a_cols, out_cols, moving, moving_cols, offset, panel, passer):
    grid_rows = lax.axis_size("row")
    my_row = lax.axis_index("row")
    out_count = a_blocks.shape[0]
    slot_total = a_blocks.shape[1] * a_blocks.shape[2]
    a_flat = a_blocks.reshape(out_count, slot_total, BS, BS)
    a_cflat = a_cols.reshape(out_count, slot_total)
    tile_rows = moving.shape[0]
    start_sum = jnp.zeros((out_count, SPG, BS, BS), jnp.float32)

    def contribute(running, pieces, piece_cols, step_index):
        source = (my_row - step_index) % grid_rows
        wanted = source * panel + offset + jnp.arange(tile_rows, dtype=jnp.int32)
        hits = (a_cflat[:, :, None] == wanted[None, None, :]).astype(jnp.float32)
        stacked = jnp.einsum("nst,nsxy->tnxy", hits, a_flat, precision=EXACT)
        matches = (piece_cols[:, None, None, :] == out_cols[None, :, :, None]).astype(jnp.float32)

        def one_tile_row(total, items):
            left_side, right_side, pairing = items
            products = jnp.einsum("nxy,byz->nbxz", left_side, right_side, precision=EXACT)
            return (total + jnp.einsum("njb,nbxz->njxz", pairing, products, precision=EXACT), 0)

        running, unused = lax.scan(one_tile_row, running, (stacked, pieces, matches))
        return running

    def turn(step_index, carry):
        running, pieces, piece_cols = carry
        running = contribute(running, pieces, piece_cols, step_index)
        pieces, piece_cols = passer(pieces, piece_cols)
        return (running, pieces, piece_cols)

    running, pieces, piece_cols = lax.fori_loop(
        0, grid_rows - 1, turn, (start_sum, moving, moving_cols)
    )
    return contribute(running, pieces, piece_cols, grid_rows - 1)


def pass_whole(pieces, piece_cols):
    return shifted((pieces, piece_cols), "row", 1)


def on_device(blocks, columns, branch):
    panel = blocks.shape[0]
    layer_count = lax.axis_size("depth")
    layer = lax.axis_index("depth")
    my_row = lax.axis_index("row")
    rows_half = panel // layer_count
    first_row = layer * rows_half
    own_blocks = blocks[:, 0]
    own_cols = columns[:, 0]
    half_blocks = lax.dynamic_slice_in_dim(blocks, first_row, rows_half, 0)
    half_cols = lax.dynamic_slice_in_dim(columns, first_row, rows_half, 0)
    a_blocks, a_cols = (
        lax.all_gather(half_blocks, "col", axis=1, tiled=True),
        lax.all_gather(half_cols, "col", axis=1, tiled=True),
    )
    partial_sum = cannon_sum(
        a_blocks, a_cols, half_cols[:, 0], own_blocks, own_cols, 0, panel, pass_whole
    )
    product = lax.all_gather(partial_sum, "depth", axis=0, tiled=True)
    chooser = (branch == 1)[:, None, None, None]
    updated = jnp.where(chooser, product, 2.0 * own_blocks - product)
    row_ids = my_row * panel + jnp.arange(panel, dtype=jnp.int32)
    on_diag = (own_cols == row_ids[:, None]).astype(jnp.float32)
    old_term = jnp.sum(on_diag * jnp.trace(own_blocks, axis1=2, axis2=3))
    new_term = jnp.sum(on_diag * jnp.trace(updated, axis1=2, axis2=3))
    traces = lax.psum(jnp.stack([old_term, new_term]), ("row", "col"))
    return (updated[:, None], traces)


MESH = pl.DeviceIdType.MESH
PIECES = 6
WHOLE = 2
CHUNKS = 3


def halves(value):
    high = value.astype(jnp.bfloat16)
    return high, (value - high.astype(jnp.float32)).astype(jnp.bfloat16)


def square_kernel(
    cols_ref, branch_ref, blocks_hbm, out_ref, trace_ref,
    mine, others, tile, left, right, extra, high_ref, low_ref, total, partial, partial_in, pair, hint, hint_in, parts,
    in_sem, cross_s, cross_r, up_s, up_r, down_s, down_r, part_s, part_r,
    near_s, near_r, far_s, far_r, give_s, give_r, lift_s, lift_r,
    near_ss, near_sr, far_ss, far_sr, give_ss, give_sr, own_ss, own_sr, lift_ss, lift_sr,
    out_s, out_r, hint_s, hint_r, pair_s, pair_r, t_send, t_recv, ready,
):
    row, col, depth = lax.axis_index("row"), lax.axis_index("col"), lax.axis_index("depth")
    panel, slots = 2 * mine.shape[0], mine.shape[1]
    groups = parts.shape[0]
    size = tile.shape[0]
    half = size // 2
    piece = half // PIECES
    per_block = BS // piece
    side = col // 2

    def mirrored(value):
        return value + side * (3 - 2 * value)

    mrow, mcol = mirrored(row), mirrored(col)
    outer = mcol == 0
    end, mid, mid2, end2 = mirrored(0), mirrored(1), mirrored(2), mirrored(3)
    group1 = jnp.where(mrow == 0, end2, mid2)
    group2 = jnp.where(mrow == 0, mid2, end2)
    direct = jnp.where(mrow < 2, group1, mid)
    summed = jnp.where(mrow < 2, mid, group1)
    x_row, y_row, corner = row + 1 - 2 * (row % 2), (row + 2) % 4, 3 - row
    mrow_x, mrow_y = mrow + 1 - 2 * (mrow % 2), (mrow + 2) % 4
    beside = (x_row, y_row)
    sibling = (row, col, 1 - depth)
    plane = ((x_row, col, depth), (y_row, col, depth))
    partner = (row, col + 1 - 2 * (col % 2), depth)
    opposite = (row, 3 - col, depth)

    barrier = pltpu.get_barrier_semaphore()
    for peer in (sibling,) + plane + (partner,):
        pl.semaphore_signal(barrier, inc=1, device_id=peer, device_id_type=MESH)

    @pl.when(jnp.logical_not(outer))
    def _():
        pl.semaphore_signal(barrier, inc=1, device_id=opposite, device_id_type=MESH)

    def incoming(turn):
        block = 2 * (turn % CHUNKS) + (depth + turn // CHUNKS) % 2
        place = mine if turn < CHUNKS else others
        return block, pltpu.make_async_copy(blocks_hbm.at[block, 0], place.at[turn % CHUNKS], in_sem.at[turn])

    def ordered(turn):
        block = incoming(turn)[0]
        place = mine if turn < CHUNKS else others
        at = pl.ds(pl.multiple_of(block * BS, BS), BS)
        for target_slot in range(slots):
            source = 0
            for slot in range(1, slots):
                source = jnp.where(lax.rem(cols_ref[block, 0, slot], slots) == target_slot, slot, source)
            value = place[turn % CHUNKS, source]
            tile[at, target_slot * BS:(target_slot + 1) * BS] = value
            if turn < CHUNKS:
                left[col, turn * BS:(turn + 1) * BS, target_slot * BS:(target_slot + 1) * BS] = value

    def take_blocks(turns):
        for turn in turns:
            incoming(turn)[1].wait()
        for turn in turns:
            ordered(turn)

    for turn in range(CHUNKS):
        incoming(turn)[1].start()
    for turn in range(CHUNKS):
        incoming(turn)[1].wait()
    for turn in range(CHUNKS, panel):
        incoming(turn)[1].start()
    ordered(0)
    pl.semaphore_wait(barrier, jnp.where(outer, 4, 5))

    def copy(src, dst, send, recv, target):
        return pltpu.make_async_remote_copy(
            src_ref=src, dst_ref=dst, send_sem=send, recv_sem=recv, device_id=target, device_id_type=MESH
        )

    def some(index, count=1):
        return pl.ds(pl.multiple_of(index * piece, piece), count * piece)

    def spot(index, core):
        start = (2 * (index // per_block) + core) * BS + (index % per_block) * piece
        return pl.ds(pl.multiple_of(start, piece), piece)

    def chunk(index, core):
        return pl.ds(pl.multiple_of((2 * index + core) * BS, BS), BS)

    def cross(which, index):
        place = left.at[col if which == 0 else end, some(index)]
        return copy(place, place, cross_s.at[which, index], cross_r.at[which, index], opposite)

    def cross_in(second, index):
        which = jnp.where((mrow == 0) != second, 1, 0)
        place = left.at[group2 if second else group1, some(index)]
        return copy(place, place, cross_s.at[which, index], cross_r.at[which, index], sibling)

    def up(index):
        place = left.at[end, some(index)]
        return copy(place, place, up_s.at[index], up_r.at[index], partner)

    def down(which, index):
        place = left.at[(mid, group1, group2)[which], some(index)]
        return copy(place, place, down_s.at[which, index], down_r.at[which, index], partner)

    def goes_down(which, index):
        whole = index < WHOLE
        if which == 2:
            return whole
        return jnp.logical_or(whole, mrow >= 2 if which == 0 else mrow < 2)

    def down_part(index):
        at = some(index)
        return copy(partial.at[at], partial_in.at[at], part_s.at[index], part_r.at[index], partner)

    def near(axis, index):
        at = chunk(index, depth)
        return copy(tile.at[at], right.at[row, at], near_s.at[axis, index], near_r.at[axis, index], plane[axis])

    def near_place(axis, index, core):
        place = right.at[beside[axis], chunk(index, core)]
        return place, copy(place, place, near_ss.at[axis, index], near_sr.at[axis, index], sibling)

    def far(axis, index):
        place = right.at[beside[1 - axis], spot(index, depth)]
        return copy(place, place, far_s.at[axis, index], far_r.at[index], plane[axis])

    def goes_far(axis, index):
        who = (mrow_x, mrow_y)[axis]
        turn, part = index // per_block, index % per_block
        by_x = turn == 0 or (turn == CHUNKS - 1 and part == 0)
        mixed = jnp.logical_or(outer, who == 0)
        if by_x == (axis == 0):
            return jnp.logical_or(mixed, who == 1 if axis == 0 else who >= 2)
        return jnp.logical_and(jnp.logical_not(mixed), who == 1 if axis == 0 else who >= 2)

    def far_place(index, core):
        place = right.at[corner, spot(index, core)]
        return place, copy(place, place, far_ss.at[index], far_sr.at[index], sibling)

    def parts_of(turn):
        return range(per_block * turn, per_block * (turn + 1))

    def take_near(axis, index, forward=True):
        place, share = near_place(axis, index, depth)
        copy(place, place, near_s.at[axis, index], near_r.at[axis, index], sibling).wait_recv()
        share.start()
        if forward:
            pass_far(1 - axis, index)

    def pass_far(axis, turn):
        for index in parts_of(turn):
            @pl.when(goes_far(axis, index))
            def _(index=index):
                far(axis, index).start()

    def take_far(turn):
        for index in parts_of(turn):
            place, share = far_place(index, depth)
            copy(place, place, far_s.at[0, index], far_r.at[index], sibling).wait_recv()
            share.start()

    def far_shared(turn):
        for index in parts_of(turn):
            far_place(index, 1 - depth)[1].wait_recv()

    x_slot = jnp.where(mrow == 2, 1, 0)
    x_slot_there = jnp.where(mrow_x == 2, 1, 0)
    own_slot = jnp.where(mrow == 3, 1, 0)

    def give(axis, index):
        slot = x_slot_there if axis == 0 else 1
        return copy(
            left.at[end, some(index)], extra.at[slot, spot(index, depth)],
            give_s.at[axis, index], give_r.at[axis, index], plane[axis],
        )

    def lifted(who):
        return jnp.where(who == 0, 1, CHUNKS - 1)

    gives_at_all = (mrow != 0, mrow >= 2)
    given_at_all = (mrow != 1, mrow < 2)

    def gives(axis, index):
        return jnp.logical_and(gives_at_all[axis], index // per_block != lifted((mrow_x, mrow_y)[axis]))

    def given(axis, index):
        return jnp.logical_and(given_at_all[axis], index // per_block != lifted(mrow))

    def give_place(axis, index, core):
        place = extra.at[x_slot if axis == 0 else 1, spot(index, core)]
        return place, copy(place, place, give_ss.at[axis, index], give_sr.at[axis, index], sibling)

    def take_given(axis, index):
        @pl.when(given(axis, index))
        def _():
            place, share = give_place(axis, index, depth)
            copy(place, place, give_s.at[axis, index], give_r.at[axis, index], sibling).wait_recv()
            share.start()

    def own_share(index, core):
        return copy(
            left.at[end, some(index)], extra.at[own_slot, spot(index, core)],
            own_ss.at[index], own_sr.at[index], sibling,
        )

    def lift(axis):
        at = chunk(lifted(mrow), depth)
        place = extra.at[x_slot if axis == 0 else 1, at]
        return copy(right.at[beside[axis], at], place, lift_s.at[axis], lift_r.at[axis], partner)

    def lift_place(axis, core):
        place = extra.at[x_slot if axis == 0 else 1, chunk(lifted(mrow), core)]
        return place, copy(place, place, lift_ss.at[axis], lift_sr.at[axis], sibling)

    def lifts(act):
        for axis in range(2):
            @pl.when(given_at_all[axis])
            def _(axis=axis):
                act(axis)

    def split(source, slot, begin, count):
        def one(part, carry):
            at = pl.ds(pl.multiple_of((begin + part) * BS, BS), BS)
            high_ref[slot, at], low_ref[slot, at] = halves(source[at])
            return carry
        lax.fori_loop(0, count, one, 0)

    dot = functools.partial(jnp.dot, preferred_element_type=jnp.float32)

    def times(value, slot, at):
        high, low = halves(value)
        return (dot(high, low_ref[slot, at]) + dot(low, high_ref[slot, at])) + dot(high, high_ref[slot, at])

    everything = pl.ds(0, size)

    def accumulate(group, begin, count, at=everything):
        if count == CHUNKS:
            result = times(left[group, :, at], group, at)
            for slot in range(slots):
                total[slot] += result[:, slot * BS:(slot + 1) * BS]
            return

        def one(part, carry):
            rows = pl.ds(pl.multiple_of((begin + part) * BS, BS), BS)
            result = times(left[group, rows, at], group, at)
            for slot in range(slots):
                total[slot, rows] += result[:, slot * BS:(slot + 1) * BS]
            return carry
        lax.fori_loop(0, count, one, 0)

    def block_of(index):
        return 2 * (index // per_block) + depth

    def out_share(index, core):
        inner = pl.ds((index % per_block) * piece, piece)
        place = out_ref.at[2 * (index // per_block) + core, 0, :, inner]
        return copy(place, place, out_s.at[index], out_r.at[index], sibling)

    def finish(index):
        block = block_of(index)
        inner = pl.ds(pl.multiple_of((index % per_block) * piece, piece), piece)
        taken = branch_ref[block] == 1
        for slot in range(slots):
            square = total[lax.rem(cols_ref[block, 0, slot], slots), some(index)]
            out_ref[block, 0, slot, inner] = jnp.where(taken, square, 2.0 * mine[index // per_block, slot, inner] - square)
        out_share(index, depth).start()

    eye = lax.broadcasted_iota(jnp.int32, (BS, BS), 0) == lax.broadcasted_iota(jnp.int32, (BS, BS), 1)
    lane = lax.broadcasted_iota(jnp.int32, parts.shape[1:], 1)

    def old_and_new(old_sum, new_sum):
        old_all = jnp.sum(jnp.where(eye, old_sum, 0.0))
        new_all = jnp.sum(jnp.where(eye, new_sum, 0.0))
        return jnp.where(lane == 0, old_all, jnp.where(lane == 1, new_all, 0.0))

    def block_traces():
        old_sum = jnp.zeros((BS, BS), jnp.float32)
        new_sum = jnp.zeros((BS, BS), jnp.float32)
        for index in range(CHUNKS):
            block = 2 * index + depth
            at = pl.ds(pl.multiple_of(block * BS, BS), BS)
            old = tile[at, at]
            square = total[block, index * BS:(index + 1) * BS]
            new_sum += jnp.where(branch_ref[block] == 1, square, 2.0 * old - square)
            old_sum += old
        return old_and_new(old_sum, new_sum)

    def partial_traces():
        new_sum = jnp.zeros((BS, BS), jnp.float32)
        for index in range(WHOLE // per_block, CHUNKS):
            block = 2 * index + depth
            start = index * BS - WHOLE * piece
            square = partial[start:start + BS, pl.ds(pl.multiple_of(block * BS, BS), BS)]
            new_sum += jnp.where(branch_ref[block] == 1, square, -square)
        return old_and_new(jnp.zeros((BS, BS), jnp.float32), new_sum)

    def hint_copy():
        return copy(hint, hint_in, hint_s.at[0], hint_r.at[0], partner)

    def pair_copy():
        return copy(pair.at[0], pair.at[1], pair_s.at[0], pair_r.at[0], sibling)

    def t_copy(peer):
        return copy(parts.at[row], parts.at[row], t_send.at[peer], t_recv.at[row], (peer // groups, peer % groups, depth))

    def to_peers(act):
        def one(peer):
            @pl.when(peer != row * groups + col)
            def _():
                act(t_copy(peer))
        loop(0, groups * groups, one)

    def send_traces():
        pair_copy().wait_recv()
        parts[row] = pair[0] + pair[1]
        to_peers(lambda c: c.start())

    def loop(begin, end_at, body):
        def one(index, carry):
            body(index)
            return carry
        lax.fori_loop(begin, end_at, one, 0)

    def tell(stage, target):
        pl.semaphore_signal(ready.at[stage], inc=1, device_id=target, device_id_type=MESH)

    def hear(stage):
        pl.semaphore_wait(ready.at[stage], 1)

    def plane_sent():
        for axis in range(2):
            for index in range(CHUNKS):
                near(axis, index).wait_send()
                near_place(axis, index, depth)[1].wait_send()
            for index in range(PIECES):
                @pl.when(goes_far(axis, index))
                def _(axis=axis, index=index):
                    far(axis, index).wait_send()
        for index in range(PIECES):
            far_place(index, depth)[1].wait_send()

    def outer_sent():
        plane_sent()
        loop(0, PIECES, lambda i: up(i).wait_send())

        lifts(lambda axis: lift(axis).wait_send())

    def given_sent():
        def sent(index):
            for axis in range(2):
                @pl.when(gives(axis, index))
                def _(axis=axis):
                    give(axis, index).wait_send()

                @pl.when(given(axis, index))
                def _(axis=axis):
                    give_place(axis, index, depth)[1].wait_send()

            @pl.when(mrow != 0)
            def _():
                own_share(index, depth).wait_send()

        loop(0, PIECES, sent)

    def inner_sent():
        plane_sent()

        def sent(index):
            for which in range(2):
                cross(which, index).wait_send()
            for which in range(3):
                @pl.when(goes_down(which, index))
                def _(which=which):
                    down(which, index).wait_send()

        loop(0, PIECES, sent)
        loop(0, PIECES - WHOLE, lambda i: down_part(i).wait_send())
        lifts(lambda axis: lift_place(axis, depth)[1].wait_send())

    def near_ready(axis, begin, end_at):
        for index in range(begin, end_at):
            near_place(axis, index, 1 - depth)[1].wait_recv()
        split(right.at[beside[axis]], beside[axis], 2 * begin, 2 * (end_at - begin))

    def near_part(axis, begin, end_at):
        near_ready(axis, begin, end_at)
        accumulate(beside[axis], 0, CHUNKS, pl.ds(2 * begin * BS, 2 * (end_at - begin) * BS))

    @pl.when(outer)
    def _():
        def rest_up():
            loop(PIECES - per_block, PIECES, lambda i: up(i).start())

        for index in range(CHUNKS):
            if index:
                ordered(index)
            if index < CHUNKS - 1:
                loop(per_block * index, per_block * (index + 1), lambda i: up(i).start())
            else:
                pl.when(mrow != 0)(rest_up)
            for axis in range(2):
                near(axis, index).start()
        tell(0, plane[0])
        take_blocks(range(CHUNKS, panel))
        total[...] = jnp.zeros_like(total)
        split(tile, row, 0, panel)
        for index in range(CHUNKS):
            for axis in range(2):
                take_near(axis, index)
            if index == 0:
                hear(0)
                tell(1, plane[1])
            if index == 1:
                @pl.when(mrow == 0)
                def _():
                    lifts(lambda axis: lift(axis).start())
                    rest_up()

                hear(1)
                tell(2, partner)

        @pl.when(mrow != 0)
        def _():
            lifts(lambda axis: lift(axis).start())

        for index in range(CHUNKS):
            for axis in range(2):
                near_place(axis, index, 1 - depth)[1].wait_recv()
        for axis in range(2):
            split(right.at[beside[axis]], beside[axis], 0, panel)
        for index in range(CHUNKS):
            take_far(index)
        for index in range(CHUNKS):
            far_shared(index)
        split(right.at[corner], corner, 0, panel)
        accumulate(end, 0, CHUNKS)

        def arrived(which, index):
            @pl.when(goes_down(which, index))
            def _():
                place = left.at[(mid, group1, group2)[which], some(index)]
                copy(place, place, down_s.at[which, index], down_r.at[which, index], sibling).wait_recv()

        for which in range(3):
            loop(0, PIECES, lambda i: arrived(which, i))
            if which == 1:
                accumulate(direct, 0, CHUNKS)
                accumulate(summed, 0, 1)
        accumulate(group2, 0, 1)
        loop(0, WHOLE, finish)

        @pl.when(mrow == 0)
        def _():
            hint[...] = block_traces()
            hint_copy().start()

        def last(index):
            at = some(index)
            place = partial_in.at[at]
            copy(place, place, part_s.at[index], part_r.at[index], sibling).wait_recv()
            value = partial_in[at]
            for slot in range(slots):
                total[slot, some(index + WHOLE)] += value[:, slot * BS:(slot + 1) * BS]
            finish(index + WHOLE)

        outer_sent()
        loop(0, PIECES - WHOLE, last)
        pl.when(mrow == 0)(lambda: hint_copy().wait_send())

    @pl.when(jnp.logical_not(outer))
    def _():
        for index in range(CHUNKS):
            first_piece, last_piece = per_block * index, per_block * (index + 1)
            if index:
                ordered(index)

            def own_cross():
                loop(first_piece, last_piece, lambda i: cross(0, i).start())

            def own_down():
                loop(first_piece, last_piece, lambda i: down(0, i).start())

            if last_piece <= WHOLE:
                own_cross()
                own_down()
            else:
                pl.when(mrow != 3)(own_cross)
                pl.when(mrow >= 2)(own_down)
            for axis in range(2):
                if index:
                    pl.when(jnp.logical_not(gives_at_all[axis]))(lambda: near(axis, index).start())
                else:
                    near(axis, index).start()
        tell(0, plane[0])
        take_blocks(range(CHUNKS, panel))
        total[...] = jnp.zeros_like(total)
        split(tile, row, 0, panel)

        mrow_there = (mrow_x, mrow_y)

        def pass_up(index):
            up(index).wait_recv()
            cross(1, index).start()

        def first(index):
            @pl.when(jnp.logical_or(mrow != 0, index < PIECES - per_block))
            def _():
                pass_up(index)

            for axis in range(2):
                @pl.when(gives(axis, index))
                def _(axis=axis):
                    give(axis, index).start()

                for turn in range(1, CHUNKS):
                    moment = jnp.where(mrow_there[axis] == 0, (1, 5)[turn - 1], 3)

                    @pl.when(jnp.logical_and(gives_at_all[axis], index == moment))
                    def _(axis=axis, turn=turn):
                        near(axis, turn).start()

            @pl.when(mrow != 0)
            def _():
                own_share(index, depth).start()

            cross_in(False, index).wait_recv()

            @pl.when(goes_down(1, index))
            def _():
                down(1, index).start()

            @pl.when(index == 1)
            def _():
                for axis in range(2):
                    take_near(axis, 0, False)
                for axis in range(2):
                    pl.when(jnp.logical_not(gives_at_all[axis]))(functools.partial(pass_far, axis, 0))

            @pl.when(jnp.logical_and(mrow == 0, index == PIECES - 2))
            def _():
                for axis in range(2):
                    take_near(axis, 1)

            @pl.when(index >= 2)
            def _():
                for axis in range(2):
                    take_given(axis, index - 2)

        def whole_group2(index):
            cross_in(True, index).wait_recv()
            down(2, index).start()

        pl.when(mrow == 0)(lambda: loop(0, WHOLE, whole_group2))
        loop(0, PIECES, first)

        @pl.when(mrow == 3)
        def _():
            loop(WHOLE, PIECES, lambda i: cross(0, i).start())

        for axis in range(2):
            pl.when(gives_at_all[axis])(functools.partial(pass_far, axis, 0))
        hear(0)
        tell(1, plane[1])
        early = (mrow == 1, mrow >= 2)
        for axis in range(2):
            @pl.when(early[axis])
            def _(axis=axis):
                for turn in range(1, CHUNKS):
                    take_near(axis, turn)

        @pl.when(jnp.logical_or(mrow == 1, mrow == 2))
        def _():
            accumulate(row, 0, CHUNKS)

        @pl.when(mrow == 3)
        def _():
            near_part(1, 0, CHUNKS)

        for index in range(WHOLE):
            pl.when(mrow != 0)(functools.partial(whole_group2, index))
            for axis in range(2):
                take_given(axis, PIECES - 2 + index)

        def take_lift(axis):
            place, share = lift_place(axis, depth)
            copy(place, place, lift_s.at[axis], lift_r.at[axis], sibling).wait_recv()
            share.start()

        def shared(index):
            for axis in range(2):
                @pl.when(given(axis, index))
                def _(axis=axis):
                    give_place(axis, index, 1 - depth)[1].wait_recv()

            @pl.when(mrow != 0)
            def _():
                own_share(index, 1 - depth).wait_recv()

        loop(0, PIECES, shared)

        @pl.when(mrow != 0)
        def _():
            for index in range(CHUNKS):
                extra[own_slot, chunk(index, depth)] = left[end, index * BS:(index + 1) * BS]

        def split_extra(slot, turn):
            split(extra.at[slot], groups + slot, 2 * turn, 2)

        from_z = (
            (mrow == 0, 0, 1), (mrow == 0, 1, 1), (mrow == 3, 0, CHUNKS - 1),
            (jnp.logical_or(mrow == 1, mrow == 2), 1, CHUNKS - 1),
        )
        for slot in range(2):
            for turn in range(CHUNKS):
                late = [condition for condition, *which in from_z if which == [slot, turn]]
                if late:
                    pl.when(jnp.logical_not(late[0]))(functools.partial(split_extra, slot, turn))
                else:
                    split_extra(slot, turn)

        later_rows = slice(WHOLE * piece, None)

        def begin_part(begin, end_at, add=True):
            at = pl.ds(2 * begin * BS, 2 * (end_at - begin) * BS)
            result = times(left[summed, later_rows, at], groups, at)
            partial[...] = partial[...] + result if add else result

        @pl.when(jnp.logical_or(mrow == 1, mrow == 2))
        def _():
            begin_part(0, CHUNKS, False)

        @pl.when(mrow == 3)
        def _():
            begin_part(0, 2, False)

        @pl.when(mrow == 0)
        def _():
            begin_part(0, 1, False)
            begin_part(2, CHUNKS)

        given_sent()
        lifts(take_lift)
        lifts(lambda axis: lift_place(axis, 1 - depth)[1].wait_recv())
        for condition, slot, turn in from_z:
            pl.when(condition)(functools.partial(split_extra, slot, turn))
        pl.when(mrow == 0)(lambda: begin_part(1, 2))
        pl.when(mrow == 3)(lambda: begin_part(2, CHUNKS))
        hear(1)

        def send_part(index):
            cross_in(True, index).wait_recv()
            at = some(index - WHOLE)
            partial[at] += times(left[group2, some(index)], groups + 1, everything)
            down_part(index - WHOLE).start()

        def corner_part(turn):
            take_far(turn)
            far_shared(turn)
            split(right.at[corner], corner, 2 * turn, 2)
            if turn < CHUNKS - 1:
                accumulate(corner, 0, CHUNKS, pl.ds(2 * turn * BS, 2 * BS))

        send_part(WHOLE)
        pl.when(mrow == 0)(lambda: pass_up(PIECES - 2))
        for axis in range(2):
            @pl.when(jnp.logical_and(mrow != 0, jnp.logical_not(early[axis])))
            def _(axis=axis):
                take_near(axis, 1)

        @pl.when(mrow == 0)
        def _():
            near_part(0, 0, 2)
            accumulate(row, 0, 1)

        @pl.when(mrow == 1)
        def _():
            near_part(0, 0, CHUNKS)

        @pl.when(mrow == 2)
        def _():
            near_part(1, 0, CHUNKS)

        @pl.when(mrow == 3)
        def _():
            near_part(0, 0, 2)

        hear(2)
        tell(3, opposite)
        send_part(WHOLE + 1)
        pl.when(mrow == 0)(lambda: pass_up(PIECES - 1))
        for axis in range(2):
            @pl.when(jnp.logical_not(early[axis]))
            def _(axis=axis):
                take_near(axis, 2)

        @pl.when(mrow == 0)
        def _():
            accumulate(row, 1, 2)

        @pl.when(jnp.logical_or(mrow == 0, mrow == 3))
        def _():
            near_part(0, 2, CHUNKS)

        @pl.when(mrow != 0)
        def _():
            corner_part(0)

        send_part(WHOLE + 2)
        hear(3)

        @pl.when(mrow < 2)
        def _():
            near_ready(1, 0, CHUNKS)

        @pl.when(mrow == 2)
        def _():
            near_ready(0, 0, CHUNKS)

        pl.when(mrow != 0)(lambda: accumulate(group2, 0, 2))

        @pl.when(mrow != 0)
        def _():
            corner_part(1)

        send_part(WHOLE + 3)

        @pl.when(mrow == 0)
        def _():
            copy(hint, hint_in, hint_s.at[0], hint_r.at[0], sibling).wait_recv()
            pair[0] = partial_traces() + hint_in[...]
            pair_copy().start()

        pl.when(mrow != 0)(lambda: accumulate(group2, 2, 1))
        pl.when(mrow == 0)(lambda: accumulate(group2, 0, CHUNKS))

        @pl.when(mrow == 0)
        def _():
            corner_part(0)
            send_traces()
            corner_part(1)

        corner_part(2)
        at = pl.ds(2 * (CHUNKS - 1) * BS, 2 * BS)

        def last_block(index):
            accumulate(corner, index, 1, at)
            loop(per_block * index, per_block * (index + 1), finish)

        pl.when(mrow != 1)(lambda: loop(0, CHUNKS, last_block))

        @pl.when(mrow == 1)
        def _():
            accumulate(corner, 0, CHUNKS, at)
            pair[0] = block_traces()
            pair_copy().start()
            loop(0, PIECES - per_block, finish)
            send_traces()
            loop(PIECES - per_block, PIECES, finish)


    for source in range(groups):
        @pl.when(jnp.logical_or(row != source, col != min(max(source, 1), groups - 2)))
        def _(source=source):
            copy(parts.at[source], parts.at[source], t_send.at[source], t_recv.at[source], sibling).wait_recv()
    sum_all = parts[0]
    for source in range(1, groups):
        sum_all = sum_all + parts[source]
    trace_ref[...] = sum_all

    @pl.when(jnp.logical_and(jnp.logical_not(outer), mrow < 2))
    def _():
        pair_copy().wait_send()
        to_peers(lambda c: c.wait_send())

    pl.when(jnp.logical_not(outer))(inner_sent)

    def last_share(index):
        out_share(index, 1 - depth).wait_recv()
        out_share(index, depth).wait_send()

    loop(0, PIECES, last_share)


def full_rows(groups, blocks, columns, branch):
    panel, _, slots = blocks.shape[:3]
    size = panel * BS
    half = size // 2
    later = half - WHOLE * (half // PIECES)
    sems = pltpu.SemaphoreType.DMA
    vmem = pl.BlockSpec(memory_space=pltpu.VMEM)
    smem = pl.BlockSpec(memory_space=pltpu.SMEM)

    def both(*shape):
        return [sems(shape), sems(shape)]

    updated, traces = pl.pallas_call(
        square_kernel,
        out_shape=(
            pltpu.VMEM(blocks.shape, jnp.float32),
            pltpu.VMEM((8, BS), jnp.float32),
        ),
        in_specs=[smem, smem, pl.BlockSpec(memory_space=pl.ANY)],
        out_specs=(vmem, vmem),
        scratch_shapes=[
            pltpu.VMEM((panel // 2, slots, BS, BS), jnp.float32),
            pltpu.VMEM((panel // 2, slots, BS, BS), jnp.float32),
            pltpu.VMEM((size, size), jnp.float32),
            pltpu.VMEM((groups, half, size), jnp.float32),
            pltpu.VMEM((groups, size, size), jnp.float32),
            pltpu.VMEM((2, size, size), jnp.float32),
            pltpu.VMEM((groups + 2, size, size), jnp.bfloat16),
            pltpu.VMEM((groups + 2, size, size), jnp.bfloat16),
            pltpu.VMEM((slots, half, BS), jnp.float32),
            pltpu.VMEM((later, size), jnp.float32),
            pltpu.VMEM((later, size), jnp.float32),
            pltpu.VMEM((2, 8, BS), jnp.float32),
            pltpu.VMEM((8, BS), jnp.float32),
            pltpu.VMEM((8, BS), jnp.float32),
            pltpu.VMEM((groups, 8, BS), jnp.float32),
            sems((panel,)),
            *both(2, PIECES),
            *both(PIECES),
            *both(3, PIECES),
            *both(PIECES - WHOLE),
            *both(2, CHUNKS),
            sems((2, PIECES)),
            sems((PIECES,)),
            *both(2, PIECES),
            *both(2),
            *both(2, CHUNKS),
            *both(PIECES),
            *both(2, PIECES),
            *both(PIECES),
            *both(2),
            *both(PIECES),
            *both(1),
            *both(1),
            sems((groups * groups,)),
            sems((groups,)),
            pltpu.SemaphoreType.REGULAR((4,)),
        ],
        compiler_params=pltpu.CompilerParams(
            collective_id=0, has_side_effects=True, vmem_limit_bytes=60 * 2**20
        ),
    )(columns, branch, blocks)
    return updated, traces[0, :2]


def solution(mesh):
    placed = (P("row", "col", None, None, None), P("row", "col", None), P("row"))
    grid = mesh.shape["row"], mesh.shape["col"], mesh.shape["depth"]

    def per_device(blocks, columns, branch):
        panel, _, slots = blocks.shape[:3]
        if grid[0] == 4 and grid[1] == 4 and grid[2] == 2 and panel == slots == 2 * CHUNKS:
            return full_rows(grid[1], blocks, columns, branch)
        return on_device(blocks, columns, branch)

    return jax.shard_map(
        per_device,
        mesh=mesh,
        in_specs=placed,
        out_specs=(P("row", "col", None, None, None), P()),
        check_vma=False,
    )
```
